32 devices in a mesh: dp: 8 (over z, x), mp: 4 (over y, core).
Axes of the slice: x: 2, y: 2, z: 4, core: 2. Of those that a mesh axis runs over, the one named last changes fastest.
Arguments:
- tokens: bfloat16 [4096, 768], P(('dp', 'mp')), may hold values from -6 to 6
- cotangent: bfloat16 [4096, 768], P(('dp', 'mp')), may hold values from -6 to 6
- attn_gain: bfloat16 [768], P('dp'), may hold values from 0.25 to 1.75
- w_qkv: bfloat16 [768, 3, 768], P('dp', None, 'mp'), as said below
- w_attn_out: bfloat16 [768, 768], P('mp', 'dp'), may hold values from -2.5 to 2.5
- mlp_gain: bfloat16 [768], P('dp'), may hold values from 0.25 to 1.75
- w_in: bfloat16 [768, 2, 1152], P('dp', None, 'mp'), may hold values from -0.21875 to 0.21875
- w_mlp_out: bfloat16 [1152, 768], P('mp', 'dp'), may hold values from -0.1875 to 0.1875
Outputs:
- output: float32 [4096, 768], P(('dp', 'mp'))
- tokens_grad: float32 [4096, 768], P(('dp', 'mp'))
- attn_gain_grad: float32 [768], P('dp')
- w_qkv_grad: float32 [768, 3, 768], P('dp', None, 'mp')
- w_attn_out_grad: float32 [768, 768], P('mp', 'dp')
- mlp_gain_grad: float32 [768], P('dp')
- w_in_grad: float32 [768, 2, 1152], P('dp', None, 'mp')
- w_mlp_out_grad: float32 [1152, 768], P('mp', 'dp')
The draws below stay inside these ranges and needn't reach their ends.
Inputs may be any that keep to these rules, and one draw needn't show every extreme that they name: Entries of w_qkv lie within plus or minus 8 / sqrt(768).
All inputs are finite; a program needn't handle non-finite values.
Results may differ from the reference program's by a relative error of at most 0.015.
Values may be sent and summed in bfloat16 or wider, within the bound.
A program may use at most 64 MiB of HBM per device.

```python
import jax
import jax.numpy as jnp
from jax import lax

D = 768
HEADS = 12
FF = 1152
HEAD_DIM = 64
SEQ_LEN = 512
TOKENS = 4096
N_DP = 8


def draw_w_qkv(key, part):
    values = jnp.clip(jax.random.normal(key, (D, 3, D), jnp.float32), -8.0, 8.0)
    return (values * D ** (-0.5)).astype(jnp.bfloat16)


def raised(values, rng, source, target, blocks, factor):
    owner, partner = [(jnp.arange(values.shape[dim]) // (values.shape[dim] // blocks)).reshape([-1 if axis == dim else 1 for axis in range(values.ndim)]) for dim in (source, target)]
    chosen = jax.random.permutation(rng, blocks)[partner]
    strong = (owner == chosen) | (owner == (partner + blocks // 2) % blocks)
    return jnp.where(strong, factor * values, values)


def levels(rng, shape, shards, least, largest):
    factor_of, own = 1.0, jax.random.fold_in(rng, 6)
    for axis_at, blocks in shards:
        heights = jnp.exp(jax.random.uniform(jax.random.fold_in(own, axis_at), (blocks,), jnp.float32, least / len(shards), largest / len(shards)))
        factor_of = factor_of * jnp.repeat(heights, shape[axis_at] // blocks).reshape([-1 if axis == axis_at else 1 for axis in range(len(shape))])
    return factor_of


def centred(key, extent, scale, bound, split=(), held_as=jnp.bfloat16):
    factor_of = levels(key, extent, split, -0.22, 0.18) if split else 1.0
    result = jax.random.normal(key, extent, jnp.float32) * scale * factor_of
    return jnp.minimum(jnp.maximum(result, -bound), bound).astype(held_as)


def heavy_noise(rng, shape, spread, most, shards, heavy, kind=jnp.bfloat16):
    entries = spread * jax.random.normal(rng, shape, jnp.float32)
    if shards:
        entries = entries * levels(rng, shape, shards, -0.22, 0.18)
    return jnp.clip(raised(entries, jax.random.fold_in(rng, 3), *heavy), -most, most).astype(kind)


def setup_inputs(seed: int = 0) -> dict:
    key_of = jax.random.split(jax.random.key(seed), 9)
    return {
        "tokens": heavy_noise(key_of[0], (TOKENS, D), 1.0, 6.0, ((0, 32),), (0, 1, 32, 2.75)),
        "cotangent": heavy_noise(key_of[1], (TOKENS, D), 1.0, 6.0, ((0, 32),), (0, 1, 32, 2.75)),
        "attn_gain": jnp.clip(1.0 + 0.15 * jax.random.normal(key_of[2], (D,), jnp.float32), 0.25, 1.75).astype(jnp.bfloat16),
        "w_qkv": draw_w_qkv(jax.random.fold_in(key_of[8], 71), 0),
        "w_attn_out": centred(key_of[4], (D, D), (max(1, D * 4 // SEQ_LEN)) ** -0.5, 2.5, ((0, 4), (1, 8))),
        "mlp_gain": jnp.clip(1.0 + 0.15 * jax.random.normal(key_of[5], (D,), jnp.float32), 0.25, 1.75).astype(jnp.bfloat16),
        "w_in": centred(key_of[6], (D, 2, FF), D ** -0.5, 0.21875, ((0, 8), (2, 4))),
        "w_mlp_out": centred(key_of[7], (FF, D), FF ** -0.5, 0.1875, ((0, 4), (1, 8))),
    }


norm_eps = 1e-05
rope_base = 160000.0
query_block = 512

def rotary_tables(length, head_width):
    half_width = head_width // 2
    freqs = rope_base ** (-(jnp.arange(half_width, dtype=jnp.float32) * 2.0 / head_width))
    angles = jnp.arange(length, dtype=jnp.float32)[:, None] * freqs[None, :]
    angles = jnp.concatenate([angles, angles], axis=1)
    return (jnp.cos(angles), jnp.sin(angles))

def rotate_half(values):
    half_width = values.shape[-1] // 2
    return jnp.concatenate([-values[..., half_width:], values[..., :half_width]], axis=-1)

def apply_rotary(values, cosine_table, sine_table):
    return values * cosine_table[:, None, :] + rotate_half(values) * sine_table[:, None, :]

def undo_rotary(grads, cosine_table, sine_table):
    return grads * cosine_table[:, None, :] - rotate_half(grads * sine_table[:, None, :])

def norm_stats(values):
    centered = values - lax.optimization_barrier(jnp.mean(values, axis=-1, keepdims=True))
    variance = lax.optimization_barrier(jnp.mean(centered * centered, axis=-1, keepdims=True))
    inverse = lax.rsqrt(variance + norm_eps)
    return (centered * inverse, inverse)

def norm_backward(grad_out, normed, inverse, gain_vals):
    scaled = grad_out * gain_vals
    grad_in = inverse * (scaled - lax.optimization_barrier(jnp.mean(scaled, axis=-1, keepdims=True)) - normed * lax.optimization_barrier(jnp.mean(scaled * normed, axis=-1, keepdims=True)))
    return (grad_in, lax.optimization_barrier(jnp.sum(grad_out * normed, axis=0)))

def gelu_exact(values):
    return 0.5 * values * (1.0 + jax.scipy.special.erf(values * 0.7071067811865476))

def gelu_slope(values):
    return 0.5 * (1.0 + jax.scipy.special.erf(values * 0.7071067811865476)) + values * jnp.exp(-0.5 * values * values) * 0.3989422804014327

def mixing(form, left, right):
    return jnp.einsum(form, left.astype(jnp.float32), right.astype(jnp.float32))

def attention_forward(queries, key_rows, value_rows):
    length, head_count, head_width = queries.shape
    block_size = min(query_block, length)
    score_scale = head_width ** (-0.5)
    blocks = queries.reshape(length // block_size, block_size, head_count, head_width)

    def one_block(block_rows):
        scores = mixing('qhd,khd->hqk', block_rows, key_rows) * score_scale
        row_peak = lax.optimization_barrier(jnp.max(scores, axis=-1, keepdims=True))
        exp_scores = jnp.exp(scores - row_peak)
        row_total = lax.optimization_barrier(jnp.sum(exp_scores, axis=-1, keepdims=True))
        attn_probs = (exp_scores / row_total).astype(jnp.bfloat16)
        block_out = mixing('hqk,khd->qhd', attn_probs, value_rows)
        return (block_out.astype(jnp.bfloat16), (row_peak + jnp.log(row_total))[..., 0])
    outs, log_totals = lax.map(one_block, blocks)
    return (outs.reshape(length, head_count, head_width), log_totals)

def attention_backward(queries, key_rows, value_rows, attended, log_totals, grad_out):
    length, head_count, head_width = queries.shape
    block_size = min(query_block, length)
    nblocks = length // block_size
    score_scale = head_width ** (-0.5)

    def one_block(running, block_inputs):
        key_grad, value_grad = running
        block_rows, out_rows, grad_rows, lse_rows = block_inputs
        scores = mixing('qhd,khd->hqk', block_rows, key_rows) * score_scale
        attn_probs = jnp.exp(scores - lse_rows[..., None])
        value_grad = value_grad + mixing('hqk,qhd->khd', attn_probs.astype(jnp.bfloat16), grad_rows)
        dprobs = mixing('qhd,khd->hqk', grad_rows, value_rows)
        row_delta = lax.optimization_barrier(jnp.sum(grad_rows.astype(jnp.float32) * out_rows.astype(jnp.float32), axis=-1)).T
        dscores = (attn_probs * (dprobs - row_delta[..., None]) * score_scale).astype(jnp.bfloat16)
        query_grad = mixing('hqk,khd->qhd', dscores, key_rows)
        key_grad = key_grad + mixing('hqk,qhd->khd', dscores, block_rows)
        return ((key_grad, value_grad), query_grad)
    zero_grad = jnp.zeros((length, head_count, head_width), jnp.float32)
    shape_blocks = (nblocks, block_size, head_count, head_width)
    block_inputs = (queries.reshape(shape_blocks), attended.reshape(shape_blocks), grad_out.reshape(shape_blocks), log_totals)
    (key_grad, value_grad), query_grad = lax.scan(one_block, (zero_grad, zero_grad), block_inputs)
    return (query_grad.reshape(length, head_count, head_width), key_grad, value_grad)

def one_sequence(seq_rows, seq_cot, attn_gain, w_qkv, w_attn_out, mlp_gain, w_in, w_mlp_out):
    length = seq_rows.shape[0]
    cosine_table, sine_table = rotary_tables(length, HEAD_DIM)
    residual = seq_rows.astype(jnp.float32)
    normed_one, inverse_one = norm_stats(residual)
    first_in = (normed_one * attn_gain.astype(jnp.float32)).astype(jnp.bfloat16)
    qkv_flat = w_qkv.reshape(D, 3 * D)
    projected = jnp.dot(first_in, qkv_flat, preferred_element_type=jnp.float32).reshape(length, 3, HEADS, HEAD_DIM)
    queries = apply_rotary(projected[:, 0], cosine_table, sine_table).astype(jnp.bfloat16)
    key_rows = apply_rotary(projected[:, 1], cosine_table, sine_table).astype(jnp.bfloat16)
    value_rows = projected[:, 2].astype(jnp.bfloat16)
    attended, log_totals = attention_forward(queries, key_rows, value_rows)
    attended_flat = attended.reshape(length, D)
    mixed_rows = residual + jnp.dot(attended_flat, w_attn_out, preferred_element_type=jnp.float32)
    normed_two, inverse_two = norm_stats(mixed_rows)
    second_in = (normed_two * mlp_gain.astype(jnp.float32)).astype(jnp.bfloat16)
    in_flat = w_in.reshape(D, 2 * FF)
    lifted = jnp.dot(second_in, in_flat, preferred_element_type=jnp.float32).reshape(length, 2, FF)
    inputs = lifted[:, 0]
    gate_vals = lifted[:, 1]
    activated = gelu_exact(inputs)
    hidden = (activated * gate_vals).astype(jnp.bfloat16)
    output = mixed_rows + jnp.dot(hidden, w_mlp_out, preferred_element_type=jnp.float32)
    hidden_grad = jnp.dot(seq_cot, w_mlp_out.T, preferred_element_type=jnp.float32)
    down_grad = jnp.dot(hidden.T, seq_cot, preferred_element_type=jnp.float32)
    input_grad = hidden_grad * gate_vals * gelu_slope(inputs)
    gate_grad = hidden_grad * activated
    lifted_grad = jnp.stack([input_grad, gate_grad], axis=1).astype(jnp.bfloat16).reshape(length, 2 * FF)
    in_grad = jnp.dot(second_in.T, lifted_grad, preferred_element_type=jnp.float32).reshape(D, 2, FF)
    second_grad = jnp.dot(lifted_grad, in_flat.T, preferred_element_type=jnp.float32)
    back_two, gain_two_grad = norm_backward(second_grad, normed_two, inverse_two, mlp_gain.astype(jnp.float32))
    mixed_grad = seq_cot.astype(jnp.float32) + back_two
    mixed_low = mixed_grad.astype(jnp.bfloat16)
    attended_grad = jnp.dot(mixed_low, w_attn_out.T, preferred_element_type=jnp.float32).astype(jnp.bfloat16).reshape(length, HEADS, HEAD_DIM)
    out_grad = jnp.dot(attended_flat.T, mixed_low, preferred_element_type=jnp.float32)
    query_grad, key_grad, value_grad = attention_backward(queries, key_rows, value_rows, attended, log_totals, attended_grad)
    query_grad = undo_rotary(query_grad, cosine_table, sine_table)
    key_grad = undo_rotary(key_grad, cosine_table, sine_table)
    projected_grad = jnp.stack([query_grad, key_grad, value_grad], axis=1).astype(jnp.bfloat16).reshape(length, 3 * D)
    qkv_grad = jnp.dot(first_in.T, projected_grad, preferred_element_type=jnp.float32).reshape(D, 3, D)
    first_grad = jnp.dot(projected_grad, qkv_flat.T, preferred_element_type=jnp.float32)
    back_one, gain_one_grad = norm_backward(first_grad, normed_one, inverse_one, attn_gain.astype(jnp.float32))
    tokens_grad = mixed_grad + back_one
    return (output, tokens_grad, (gain_one_grad, qkv_grad, out_grad, gain_two_grad, in_grad, down_grad))

def reference(tokens, cotangent, attn_gain, w_qkv, w_attn_out, mlp_gain, w_in, w_mlp_out):
    sequences = tokens.reshape(N_DP, SEQ_LEN, D)
    cot_seqs = cotangent.reshape(N_DP, SEQ_LEN, D)
    zero_sums = (jnp.zeros((D,), jnp.float32), jnp.zeros((D, 3, D), jnp.float32), jnp.zeros((D, D), jnp.float32), jnp.zeros((D,), jnp.float32), jnp.zeros((D, 2, FF), jnp.float32), jnp.zeros((FF, D), jnp.float32))

    def one_step(running, pair):
        output, tokens_grad, grads = one_sequence(pair[0], pair[1], attn_gain, w_qkv, w_attn_out, mlp_gain, w_in, w_mlp_out)
        summed = tuple((left + right for left, right in zip(running, grads)))
        return (summed, (output, tokens_grad))
    sums, (outputs, input_grads) = lax.scan(one_step, zero_sums, (sequences, cot_seqs))
    return (outputs.reshape(TOKENS, D), input_grads.reshape(TOKENS, D), sums[0], sums[1], sums[2], sums[3], sums[4], sums[5])
```

```python
import functools

import jax
import jax.numpy as jnp
import numpy as np
from jax import lax
from jax.experimental import pallas as pl
from jax.experimental.pallas import tpu as pltpu
from jax.sharding import PartitionSpec as P

MESH = pl.DeviceIdType.MESH
PAIR = 2
PARTS = 2
AHEAD = 3
BF = jnp.bfloat16
F32 = jnp.float32

HEAD_DIM = 64


norm_eps = 1e-05
rope_base = 160000.0
query_block = 512


def rotary_tables(length, head_width):
    half_width = head_width // 2
    freqs = rope_base ** (-(jnp.arange(half_width, dtype=jnp.float32) * 2.0 / head_width))
    angles = jnp.arange(length, dtype=jnp.float32)[:, None] * freqs[None, :]
    angles = jnp.concatenate([angles, angles], axis=1)
    return (jnp.cos(angles), jnp.sin(angles))


def rotate_half(values):
    half_width = values.shape[-1] // 2
    return jnp.concatenate([-values[..., half_width:], values[..., :half_width]], axis=-1)


def apply_rotary(values, cosine_table, sine_table):
    return values * cosine_table[:, None, :] + rotate_half(values) * sine_table[:, None, :]


def undo_rotary(grads, cosine_table, sine_table):
    return grads * cosine_table[:, None, :] - rotate_half(grads * sine_table[:, None, :])


def norm_stats(values):
    centered = values - jnp.mean(values, axis=-1, keepdims=True)
    variance = jnp.mean(centered * centered, axis=-1, keepdims=True)
    inverse = lax.rsqrt(variance + norm_eps)
    return (centered * inverse, inverse)


def norm_backward(grad_out, normed, inverse, gain_vals):
    scaled = grad_out * gain_vals
    grad_in = inverse * (
        scaled
        - jnp.mean(scaled, axis=-1, keepdims=True)
        - normed * jnp.mean(scaled * normed, axis=-1, keepdims=True)
    )
    return (grad_in, jnp.sum(grad_out * normed, axis=0))


def gelu_exact(values):
    return 0.5 * values * (1.0 + jax.scipy.special.erf(values * 0.7071067811865476))


def gelu_slope(values):
    return (
        0.5 * (1.0 + jax.scipy.special.erf(values * 0.7071067811865476))
        + values * jnp.exp(-0.5 * values * values) * 0.3989422804014327
    )


def contract_rows(left, right):
    return lax.dot_general(
        left, right, (((0,), (0,)), ((), ())), preferred_element_type=jnp.float32
    )


def times_transposed(left, right):
    return lax.dot_general(
        left, right, (((1,), (1,)), ((), ())), preferred_element_type=jnp.float32
    )


def attention_weights(attn_gain, w_qkv, w_attn_out):
    return (
        lax.all_gather(attn_gain, "dp", axis=0, tiled=True),
        lax.all_gather(w_qkv, "dp", axis=0, tiled=True),
        lax.all_gather(w_attn_out, "dp", axis=1, tiled=True),
    )


def feedforward_weights(mlp_gain, w_in, w_mlp_out):
    return (
        lax.all_gather(mlp_gain, "dp", axis=0, tiled=True),
        lax.all_gather(w_in, "dp", axis=0, tiled=True),
        lax.all_gather(w_mlp_out, "dp", axis=1, tiled=True),
    )


def attention_forward(queries, key_rows, value_rows):
    length, head_count, head_width = queries.shape
    block_size = min(query_block, length)
    score_scale = head_width ** (-0.5)
    blocks = queries.reshape(length // block_size, block_size, head_count, head_width)

    def one_block(block_rows):
        scores = (
            jnp.einsum("qhd,khd->hqk", block_rows, key_rows, preferred_element_type=jnp.float32)
            * score_scale
        )
        row_peak = jnp.max(scores, axis=-1, keepdims=True)
        exp_scores = jnp.exp(scores - row_peak)
        row_total = jnp.sum(exp_scores, axis=-1, keepdims=True)
        attn_probs = (exp_scores / row_total).astype(jnp.bfloat16)
        block_out = jnp.einsum(
            "hqk,khd->qhd", attn_probs, value_rows, preferred_element_type=jnp.float32
        )
        return (block_out.astype(jnp.bfloat16), (row_peak + jnp.log(row_total))[..., 0])

    outs, log_totals = lax.map(one_block, blocks)
    return (outs.reshape(length, head_count, head_width), log_totals)


def attention_backward(queries, key_rows, value_rows, attended, log_totals, grad_out):
    length, head_count, head_width = queries.shape
    block_size = min(query_block, length)
    nblocks = length // block_size
    score_scale = head_width ** (-0.5)

    def one_block(running, block_inputs):
        key_grad, value_grad = running
        block_rows, out_rows, grad_rows, lse_rows = block_inputs
        scores = (
            jnp.einsum("qhd,khd->hqk", block_rows, key_rows, preferred_element_type=jnp.float32)
            * score_scale
        )
        attn_probs = jnp.exp(scores - lse_rows[..., None])
        value_grad = value_grad + jnp.einsum(
            "hqk,qhd->khd",
            attn_probs.astype(jnp.bfloat16),
            grad_rows,
            preferred_element_type=jnp.float32,
        )
        dprobs = jnp.einsum(
            "qhd,khd->hqk", grad_rows, value_rows, preferred_element_type=jnp.float32
        )
        row_delta = jnp.sum(grad_rows.astype(jnp.float32) * out_rows.astype(jnp.float32), axis=-1).T
        dscores = (attn_probs * (dprobs - row_delta[..., None]) * score_scale).astype(jnp.bfloat16)
        query_grad = jnp.einsum(
            "hqk,khd->qhd", dscores, key_rows, preferred_element_type=jnp.float32
        )
        key_grad = key_grad + jnp.einsum(
            "hqk,qhd->khd", dscores, block_rows, preferred_element_type=jnp.float32
        )
        return ((key_grad, value_grad), query_grad)

    zero_grad = jnp.zeros((length, head_count, head_width), jnp.float32)
    shape_blocks = (nblocks, block_size, head_count, head_width)
    block_inputs = (
        queries.reshape(shape_blocks),
        attended.reshape(shape_blocks),
        grad_out.reshape(shape_blocks),
        log_totals,
    )
    (key_grad, value_grad), query_grad = lax.scan(one_block, (zero_grad, zero_grad), block_inputs)
    return (query_grad.reshape(length, head_count, head_width), key_grad, value_grad)


def shards(tokens, cotangent, attn_gain, w_qkv, w_attn_out, mlp_gain, w_in, w_mlp_out):
    gain_one, qkv_full, out_full = attention_weights(attn_gain, w_qkv, w_attn_out)
    gain_two, in_full, down_full = feedforward_weights(mlp_gain, w_in, w_mlp_out)
    model_width = tokens.shape[1]
    residual = tokens.astype(jnp.float32)
    normed_one, inverse_one = norm_stats(residual)
    first_in = (normed_one * gain_one.astype(jnp.float32)).astype(jnp.bfloat16)
    first_all = lax.all_gather(first_in, "mp", axis=0, tiled=True)
    length = first_all.shape[0]
    local_width = qkv_full.shape[2]
    head_count = local_width // HEAD_DIM
    cosine_table, sine_table = rotary_tables(length, HEAD_DIM)
    projected = jnp.dot(
        first_all,
        qkv_full.reshape(model_width, 3 * local_width),
        preferred_element_type=jnp.float32,
    )
    projected = projected.reshape(length, 3, head_count, HEAD_DIM)
    queries = apply_rotary(projected[:, 0], cosine_table, sine_table).astype(jnp.bfloat16)
    key_rows = apply_rotary(projected[:, 1], cosine_table, sine_table).astype(jnp.bfloat16)
    value_rows = projected[:, 2].astype(jnp.bfloat16)
    attended, log_totals = attention_forward(queries, key_rows, value_rows)
    attended_flat = attended.reshape(length, local_width)
    mixed_rows = residual + lax.psum_scatter(
        jnp.dot(attended_flat, out_full, preferred_element_type=jnp.float32),
        "mp",
        scatter_dimension=0,
        tiled=True,
    )
    normed_two, inverse_two = norm_stats(mixed_rows)
    second_in = (normed_two * gain_two.astype(jnp.float32)).astype(jnp.bfloat16)
    second_all = lax.all_gather(second_in, "mp", axis=0, tiled=True)
    unit_count = in_full.shape[2]
    lifted = jnp.dot(
        second_all, in_full.reshape(model_width, 2 * unit_count), preferred_element_type=jnp.float32
    )
    lifted = lifted.reshape(length, 2, unit_count)
    inputs = lifted[:, 0]
    gate_vals = lifted[:, 1]
    activated = gelu_exact(inputs)
    hidden = (activated * gate_vals).astype(jnp.bfloat16)
    output = mixed_rows + lax.psum_scatter(
        jnp.dot(hidden, down_full, preferred_element_type=jnp.float32).astype(jnp.bfloat16),
        "mp",
        scatter_dimension=0,
        tiled=True,
    ).astype(jnp.float32)
    gain_two, in_full, down_full = feedforward_weights(mlp_gain, w_in, w_mlp_out)
    gain_one, qkv_full, out_full = attention_weights(attn_gain, w_qkv, w_attn_out)
    cot_all = lax.all_gather(cotangent, "mp", axis=0, tiled=True)
    hidden_grad = times_transposed(cot_all, down_full)
    down_grad = contract_rows(hidden, cot_all)
    input_grad = hidden_grad * gate_vals * gelu_slope(inputs)
    gate_grad = hidden_grad * activated
    lifted_grad = (
        jnp.stack([input_grad, gate_grad], axis=1)
        .astype(jnp.bfloat16)
        .reshape(length, 2 * unit_count)
    )
    in_grad = contract_rows(second_all, lifted_grad).reshape(model_width, 2, unit_count)
    in_flat = in_full.reshape(model_width, 2 * unit_count)
    second_grad = lax.psum_scatter(
        times_transposed(lifted_grad, in_flat), "mp", scatter_dimension=0, tiled=True
    )
    back_two, gain_two_part = norm_backward(
        second_grad, normed_two, inverse_two, gain_two.astype(jnp.float32)
    )
    mixed_grad = cotangent.astype(jnp.float32) + back_two
    mixed_low = mixed_grad.astype(jnp.bfloat16)
    mixed_all = lax.all_gather(mixed_low, "mp", axis=0, tiled=True)
    attended_grad = (
        times_transposed(mixed_all, out_full)
        .astype(jnp.bfloat16)
        .reshape(length, head_count, HEAD_DIM)
    )
    out_grad = contract_rows(attended_flat, mixed_all)
    query_grad, key_grad, value_grad = attention_backward(
        queries, key_rows, value_rows, attended, log_totals, attended_grad
    )
    query_grad = undo_rotary(query_grad, cosine_table, sine_table)
    key_grad = undo_rotary(key_grad, cosine_table, sine_table)
    projected_grad = (
        jnp.stack([query_grad, key_grad, value_grad], axis=1)
        .astype(jnp.bfloat16)
        .reshape(length, 3 * local_width)
    )
    qkv_grad = contract_rows(first_all, projected_grad).reshape(model_width, 3, local_width)
    qkv_flat = qkv_full.reshape(model_width, 3 * local_width)
    first_grad = lax.psum_scatter(
        times_transposed(projected_grad, qkv_flat).astype(jnp.bfloat16),
        "mp",
        scatter_dimension=0,
        tiled=True,
    ).astype(jnp.float32)
    back_one, gain_one_part = norm_backward(
        first_grad, normed_one, inverse_one, gain_one.astype(jnp.float32)
    )
    tokens_grad = mixed_grad + back_one
    down_shard, in_shard, gain_two_shard, out_shard, qkv_shard, gain_one_shard = (
        lax.psum_scatter(down_grad, "dp", scatter_dimension=1, tiled=True),
        lax.psum_scatter(in_grad, "dp", scatter_dimension=0, tiled=True),
        lax.psum_scatter(gain_two_part, "dp", scatter_dimension=0, tiled=True),
        lax.psum_scatter(out_grad, "dp", scatter_dimension=1, tiled=True),
        lax.psum_scatter(qkv_grad, "dp", scatter_dimension=0, tiled=True),
        lax.psum_scatter(gain_one_part, "dp", scatter_dimension=0, tiled=True),
    )
    gain_one_grad, gain_two_grad = lax.psum((gain_one_shard, gain_two_shard), "mp")
    return (
        output,
        tokens_grad,
        gain_one_grad,
        qkv_shard,
        out_shard,
        gain_two_grad,
        in_shard,
        down_shard,
    )


def nn(left, right):
    return lax.dot_general(left, right, (((1,), (0,)), ((), ())), preferred_element_type=F32)


def nt(left, right):
    return lax.dot_general(left, right, (((1,), (1,)), ((), ())), preferred_element_type=F32)


def tn(left, right):
    return lax.dot_general(left, right, (((0,), (0,)), ((), ())), preferred_element_type=F32)


def erf(x):
    return lax.erf(x)


def swap_halves(tile):
    lane = lax.broadcasted_iota(jnp.int32, tile.shape, 1)
    half = HEAD_DIM // 2
    back = pltpu.roll(tile, tile.shape[1] - half, 1)
    ahead = pltpu.roll(tile, half, 1)
    return jnp.where(lax.rem(lane, HEAD_DIM) < half, back, ahead)


def layer_kernel(
    ndp, heads,
    tok_h, cot_h, gain_a, gain_b, wq_h, wo_h, wi_h, wd_h, cos_h, sin_h,
    out_o, tg_o, ga_o, gb_o, dq_o, do_o, di_o, dd_o,
    wq_in, wo_in, wi_in, wd_in, cos_t, sin_t,
    gpad, gains, w1, w2, wf1, wf2, wof,
    xr, x1, x2, xc, x3, xt1, xt2, xtc, xt3,
    qk, vb, att, pbuf, hid, wide, hgrad_buf, lg, pg, gatt, dqs, dks, dvs,
    xh1, xh2, mixed, mgrad,
    rs_sc, rs_rc, rs_sy, rs_ry, rs_own,
    gs1, gr1, gz1, gy1, gw1,
    gs2, gr2, gz2, gy2, gw2,
    ggs, ggr,
    send_sem, recv_sem, load_sem,
):
    nmp, rows, width = xr.shape
    length = nmp * rows
    na = ndp // PAIR
    dp = lax.axis_index("dp")
    mp = lax.axis_index("mp")
    za = dp // PAIR
    zb = lax.rem(dp, PAIR)
    core = lax.rem(mp, 2)
    ypos = mp // 2
    mate = mp + 1 - 2 * core
    ypeer = mp + 2 - 4 * ypos
    diag = mate + 2 - 4 * ypos
    xpeer = za * PAIR + (1 - zb)
    lw = heads * HEAD_DIM
    units = hid.shape[1]
    shard = w1.shape[0]
    cols_one, cols_two = w1.shape[1], w2.shape[1]

    def at_dp(d):
        return {"dp": d, "mp": mp}

    def at_mp(m):
        return {"dp": dp, "mp": m}

    counter = [0]
    sends = []

    def slot():
        counter[0] += 1
        return counter[0] - 1

    def put(src, dst, sem, dev):
        copy = pltpu.make_async_remote_copy(
            src_ref=src, dst_ref=dst, send_sem=send_sem.at[sem], recv_sem=recv_sem.at[sem],
            device_id=dev, device_id_type=MESH,
        )
        copy.start()
        sends.append(copy)

    def got(buf, sem):
        pltpu.make_async_remote_copy(
            src_ref=buf, dst_ref=buf, send_sem=send_sem.at[sem], recv_sem=recv_sem.at[sem],
            device_id=at_mp(mate), device_id_type=MESH,
        ).wait_recv()

    barrier = pltpu.get_barrier_semaphore()
    for k in range(1, ndp):
        pl.semaphore_signal(barrier, inc=1, device_id=at_dp(lax.rem(dp + k, ndp)), device_id_type=MESH)
    for other in (mate, ypeer, diag):
        pl.semaphore_signal(barrier, inc=1, device_id=at_mp(other), device_id_type=MESH)

    loads = [
        pltpu.make_async_copy(src, dst, load_sem.at[i])
        for i, (src, dst) in enumerate((
            (wq_h, wq_in), (tok_h, xr.at[mp]), (wo_h, wo_in), (wi_h, wi_in), (wd_h, wd_in),
            (cot_h, xc.at[mp]), (cos_h, cos_t), (sin_h, sin_t),
        ))
    ]
    for load in loads:
        load.start()

    def norm(vals):
        centered = vals - jnp.mean(vals, axis=-1, keepdims=True)
        inv = lax.rsqrt(jnp.mean(centered * centered, axis=-1, keepdims=True) + norm_eps)
        return centered * inv, inv

    def norm_back(grad, normed, inv, gain):
        scaled = grad * gain
        return inv * (
            scaled
            - jnp.mean(scaled, axis=-1, keepdims=True)
            - normed * jnp.mean(scaled * normed, axis=-1, keepdims=True)
        )

    def flip(vals):
        high, wide = vals.shape
        more_rows, more_cols = -high % 128, -wide % 128
        if more_cols:
            vals = jnp.concatenate([vals, jnp.zeros((high, more_cols), F32)], axis=1)
        if more_rows:
            vals = jnp.concatenate([vals, jnp.zeros((more_rows, wide + more_cols), F32)], axis=0)
        return vals.T[:wide, :high]

    def column(gain):
        row = jnp.concatenate([gain[...].astype(F32), jnp.ones((1, 128 - shard), F32)], axis=1)
        return jnp.broadcast_to(row, (128, 128)).T[:shard]

    def packed(q, k, v, o):
        parts = []
        for h in range(heads):
            parts += [q[:, h * HEAD_DIM : (h + 1) * HEAD_DIM], k[:, h * HEAD_DIM : (h + 1) * HEAD_DIM]]
        return jnp.concatenate([*parts, v, o], axis=1)

    gpad[...] = jnp.concatenate(
        [
            jnp.concatenate([gain_a[...].astype(F32), gain_b[...].astype(F32), jnp.zeros((6, shard), F32)], axis=0),
            jnp.zeros((8, 128 - shard), F32),
        ],
        axis=1,
    )
    loads[0].wait()
    loads[2].wait()
    w1[...] = packed(
        wq_in[0].astype(F32), wq_in[1].astype(F32), wq_in[2].astype(F32), flip(wo_in[...].astype(F32))
    ).astype(BF)
    loads[3].wait()
    loads[4].wait()
    w2[...] = jnp.concatenate(
        [
            wi_in[:, 0, :].astype(F32), wi_in[:, 1, :].astype(F32), flip(wd_in[...].astype(F32)),
            jnp.zeros((shard, cols_two - 3 * units), F32),
        ],
        axis=1,
    ).astype(BF)
    loads[1].wait()
    loads[5].wait()
    loads[6].wait()
    loads[7].wait()
    pl.semaphore_wait(barrier, ndp - 1 + 3)

    def gather_open(src, full, lo, hi):
        at = pl.ds(lo, hi - lo)
        return (src, full, at, [slot() for _ in range(na)], [slot() for _ in range(na)])

    def gather_far(state):
        src, full, at, zs, xs = state
        for k in (2, 1, 3):
            put(src.at[:, at], full.at[dp, :, at], zs[k], at_dp(lax.rem(za + k, na) * PAIR + zb))

    def gather_near(state):
        src, full, at, zs, xs = state
        put(src.at[:, at], full.at[dp, :, at], xs[0], at_dp(xpeer))

    def gather_forward(state, k):
        src, full, at, zs, xs = state
        source = lax.rem(za + na - k, na) * PAIR + zb
        got(full.at[source, :, at], zs[k])
        put(full.at[source, :, at], full.at[source, :, at], xs[k], at_dp(xpeer))

    def gather_end(state):
        src, full, at, zs, xs = state
        for k in range(na):
            source = lax.rem(za + na - k, na) * PAIR + (1 - zb)
            got(full.at[source, :, at], xs[k])

    order = (1, 3, 2)
    part_rows = rows // PARTS

    def part_at(p):
        return pl.ds(p * part_rows, part_rows)

    def spread_open(buf):
        return (buf, [[slot() for _ in range(3)] for _ in range(PARTS)])

    def spread_start(state, p):
        buf, sems = state
        block = buf.at[mp, part_at(p)]
        put(block, block, sems[p][0], at_mp(ypeer))
        put(block, block, sems[p][1], at_mp(mate))

    def spread_near(state):
        buf, sems = state
        for p in range(PARTS):
            got(buf.at[mate, part_at(p)], sems[p][1])

    def spread_forward(state, p):
        buf, sems = state
        block = buf.at[ypeer, part_at(p)]
        got(block, sems[p][0])
        put(block, block, sems[p][2], at_mp(mate))

    def spread_far(state):
        buf, sems = state
        for p in range(PARTS):
            got(buf.at[diag, part_at(p)], sems[p][2])

    def chunk(r):
        return pl.ds(pl.multiple_of(r * rows, rows), rows)

    def pair_rows(y):
        return pl.ds(pl.multiple_of(y * 2 * rows, 2 * rows), 2 * rows)

    near, far = pair_rows(ypos), pair_rows(1 - ypos)

    def pair_of(buf, y):
        return buf[pl.ds(pl.multiple_of(y * 2, 2), 2)].reshape(2 * rows, width)

    def scatter_open(i):
        return (i, [slot() for _ in range(PARTS)], slot(), [slot() for _ in range(PARTS)])

    def scatter_far(state, left, weights):
        i, s_far, s_near, s_y = state
        rs_sc[i, 0] = nt(left[chunk(diag), :], weights).astype(BF)
        for p in range(PARTS):
            at = part_at(p)
            put(rs_sc.at[i, 0, at], rs_rc.at[i, 0, at], s_far[p], at_mp(mate))
        rs_own[i, 0] = nt(left[chunk(ypeer), :], weights)

    def scatter_send(state):
        i, s_far, s_near, s_y = state
        for p in range(PARTS):
            at = part_at(p)
            got(rs_rc.at[i, 0, at], s_far[p])
            rs_sy[i, at, :] = (rs_own[i, 0, at, :] + rs_rc[i, 0, at, :].astype(F32)).astype(BF)
            put(rs_sy.at[i, at], rs_ry.at[i, at], s_y[p], at_mp(ypeer))

    def scatter_near(state, left, weights):
        i, s_far, s_near, s_y = state
        rs_sc[i, 1] = nt(left[chunk(mate), :], weights).astype(BF)
        put(rs_sc.at[i, 1], rs_rc.at[i, 1], s_near, at_mp(mate))
        rs_own[i, 1] = nt(left[chunk(mp), :], weights)

    def scatter_end(state, p):
        i, s_far, s_near, s_y = state
        at = part_at(p)
        if p == 0:
            got(rs_rc.at[i, 1], s_near)
        total = rs_own[i, 1, at, :] + rs_rc[i, 1, at, :].astype(F32)
        got(rs_ry.at[i, at], s_y[p])
        return total + rs_ry[i, at, :].astype(F32)

    def pairs(cols):
        cuts = [*range(0, cols - 128, 256), cols]
        return list(zip(cuts[:-1], cuts[1:]))

    def turn(buf, dst):
        @pl.loop(0, nmp)
        def _(r):
            cols = pl.ds(pl.multiple_of(r * rows, rows), rows)
            flipped = buf[r].T
            dst[:, :, :, cols] = flipped.reshape(na, PAIR, shard, rows)

    def product(xt, half, right):
        return nn(xt[:, half].reshape(na * shard, length), right).reshape(na, shard, right.shape[1])

    def grad_open(bufs, lo, hi):
        return (bufs, pl.ds(lo, hi - lo), [slot() for _ in range(na)], [slot() for _ in range(na)])

    def grad_start(state):
        (gs, gr, gz, gy, gw), at, xs, zs = state
        for k in (2, 1, 3, 0):
            a = lax.rem(za + k, na)
            put(gs.at[a, :, at], gr.at[a, :, at], xs[k], at_dp(xpeer))

    def grad_middle(state, k):
        (gs, gr, gz, gy, gw), at, xs, zs = state
        a = lax.rem(za + k, na)
        got(gr.at[a, :, at], xs[k])
        gz[k, :, at] = (gw[a, :, at] + gr[a, :, at].astype(F32)).astype(BF)
        put(gz.at[k, :, at], gy.at[k, :, at], zs[k], at_dp(a * PAIR + zb))

    def grad_end(state):
        (gs, gr, gz, gy, gw), at, xs, zs = state
        got(gr.at[za, :, at], xs[0])
        total = gw[za, :, at] + gr[za, :, at].astype(F32)
        for k in range(1, na):
            got(gy.at[k, :, at], zs[k])
            total = total + gy[k, :, at].astype(F32)
        return total

    one = (gs1, gr1, gz1, gy1, gw1)
    two = (gs2, gr2, gz2, gy2, gw2)

    gain_slots = [slot() for _ in range(ndp - 1)]
    for k in range(1, ndp):
        put(gpad, gains.at[dp], gain_slots[k - 1], at_dp(lax.rem(dp + k, ndp)))
    pieces = [gather_open(w1, wf1, c, c + 128) for c in range(0, cols_one, 128)]
    count_one = len(pieces)
    count_q = -(-3 * lw // 128)
    pieces += [gather_open(w2, wf2, c, c + 128) for c in range(0, cols_two, 128)]
    at_piece = [0]

    def pump(count):
        for _ in range(count):
            i = at_piece[0]
            if i >= len(pieces):
                return
            at_piece[0] += 1
            if i + AHEAD < len(pieces):
                gather_far(pieces[i + AHEAD])
            if i + 1 < len(pieces):
                gather_near(pieces[i + 1])
            for k in order:
                gather_forward(pieces[i], k)

    sp1 = spread_open(xr)
    gather_near(pieces[0])
    for i in range(AHEAD):
        gather_far(pieces[i])
        if i == 0:
            for p in range(PARTS):
                spread_start(sp1, p)
    gains[dp] = gpad[...]
    wf1[dp] = w1[...]
    wf2[dp] = w2[...]
    for k in range(1, ndp):
        source = lax.rem(dp + ndp - k, ndp)
        got(gains.at[source], gain_slots[k - 1])

    def whole_gain(i):
        return jnp.concatenate([gains[d, i : i + 1, :shard] for d in range(ndp)], axis=1)

    gain_one = whole_gain(0)
    gain_two = whole_gain(1)

    normed_one, inv_one = norm(xr[mp].astype(F32))
    xh1[...] = normed_one
    x1[mp] = (normed_one * gain_one).astype(BF)

    def first_norm(r):
        x1[r] = (norm(xr[r].astype(F32))[0] * gain_one).astype(BF)

    pump(1)
    spread_near(sp1)
    first_norm(mate)
    spc = spread_open(xc)
    pump(1)
    for p in range(PARTS):
        spread_forward(sp1, p)
        spread_start(spc, p)
    first_norm(ypeer)
    pump(1)
    spread_far(sp1)
    first_norm(diag)
    turn(x1, xt1)
    pump(count_q - 2)
    for p in range(PARTS):
        spread_forward(spc, p)
    for i in range(count_q):
        gather_end(pieces[i])

    wide[:, : 3 * lw] = nn(
        x1[...].reshape(length, width), wf1[:, :, : 3 * lw].reshape(width, 3 * lw)
    )

    @pl.loop(0, nmp)
    def _(r):
        at = chunk(r)
        for h in range(heads):
            t = slice(h * 128, (h + 1) * 128)
            u = wide[at, t]
            qk[at, t] = (u * cos_t[at, :] + swap_halves(u) * sin_t[at, :]).astype(BF)
        vb[at, :] = wide[at, 2 * lw : 3 * lw].astype(BF)

    scale = HEAD_DIM ** (-0.5)

    def query(h, at=slice(None)):
        return qk[at, h * 128 : h * 128 + HEAD_DIM]

    def key(h, at=slice(None)):
        return qk[at, h * 128 + HEAD_DIM : (h + 1) * 128]

    def value(h, at=slice(None)):
        return vb[at, h * HEAD_DIM : (h + 1) * HEAD_DIM]

    def attend(at):
        outs = []
        for h in range(heads):
            scores = nt(query(h, at), key(h)) * scale
            peak = jnp.max(scores, axis=-1, keepdims=True)
            e = jnp.exp(scores - peak)
            probs = e / jnp.sum(e, axis=-1, keepdims=True)
            pbuf[h, at, :] = probs
            outs.append(nn(probs.astype(BF), value(h)))
        att[at, :] = jnp.concatenate(outs, axis=1).astype(BF)

    pump(1)
    attend(far)
    pump(1)
    for i in range(count_q, count_one):
        gather_end(pieces[i])
    wof[...] = wf1[:, :, 3 * lw :].reshape(width, lw)
    rs_a = scatter_open(0)
    scatter_far(rs_a, att, wof[...])
    scatter_send(rs_a)
    attend(near)
    scatter_near(rs_a, att, wof[...])
    pump(1)
    spread_near(spc)
    spread_far(spc)
    turn(xc, xtc)
    pump(2)

    inv_two = []
    sp2 = spread_open(x2)
    for p in range(PARTS):
        at = part_at(p)
        mixed[at, :] = xr[mp, at, :].astype(F32) + scatter_end(rs_a, p)
        normed_two, inv = norm(mixed[at, :])
        inv_two.append(inv)
        xh2[at, :] = normed_two
        x2[mp, at, :] = (normed_two * gain_two).astype(BF)
        spread_start(sp2, p)
    pump(len(pieces))
    spread_near(sp2)
    for piece in pieces[count_one:]:
        gather_end(piece)

    def gelu_part(y, at):
        wide[at, : 2 * units] = nn(
            pair_of(x2, y), wf2[:, :, : 2 * units].reshape(width, 2 * units)
        )
        hgrad_buf[at, :] = nn(
            pair_of(xc, y), wf2[:, :, 2 * units : 3 * units].reshape(width, units)
        )

        @pl.loop(0, 2)
        def _(r):
            now = chunk(2 * y + r)
            u = wide[now, :units]
            gate = wide[now, units : 2 * units]
            cdf = 0.5 * (1.0 + erf(u * 0.7071067811865476))
            act = u * cdf
            slope = cdf + u * jnp.exp(-0.5 * u * u) * 0.3989422804014327
            hid[now, :] = (act * gate).astype(BF)
            hgrad = hgrad_buf[now, :]
            lg[now, :] = jnp.concatenate([hgrad * gate * slope, hgrad * act], axis=1).astype(BF)

    gelu_part(ypos, near)
    for p in range(PARTS):
        spread_forward(sp2, p)
    spread_far(sp2)
    gelu_part(1 - ypos, far)
    in_flat = wf2[:, :, : 2 * units].reshape(width, 2 * units)
    rs_g = scatter_open(1)
    scatter_far(rs_g, lg, in_flat)
    scatter_send(rs_g)
    turn(x2, xt2)
    gs2[:, :, : 2 * units] = product(xt2, 1 - zb, lg[...]).astype(BF)
    gs2[:, :, 2 * units : 3 * units] = product(xtc, 1 - zb, hid[...]).astype(BF)
    gs2[:, :, 3 * units :] = jnp.zeros((na, shard, cols_two - 3 * units), BF)
    g_two = [grad_open(two, lo, hi) for lo, hi in pairs(cols_two)]
    for g in g_two:
        grad_start(g)
    steps = [(g, k) for g in g_two for k in (2, 1, 3)]

    def reduce_steps(count):
        for _ in range(min(count, len(steps))):
            grad_middle(*steps.pop(0))

    scatter_near(rs_g, lg, in_flat)
    gw2[:, :, : 2 * units] = product(xt2, zb, lg[...])
    gw2[:, :, 2 * units : 3 * units] = product(xtc, zb, hid[...])
    gw2[:, :, 3 * units :] = jnp.zeros((na, shard, cols_two - 3 * units), F32)
    down_flat = wf2[:, :, 2 * units : 3 * units].reshape(width, units)
    rs_o = scatter_open(3)
    scatter_far(rs_o, hid, down_flat)
    scatter_near(rs_o, hid, down_flat)
    reduce_steps(2)
    sp3 = spread_open(x3)
    for p in range(PARTS):
        at = part_at(p)
        back_two = norm_back(scatter_end(rs_g, p), xh2[at, :], inv_two[p], gain_two)
        mgrad[at, :] = xc[mp, at, :].astype(F32) + back_two
        x3[mp, at, :] = mgrad[at, :].astype(BF)
        spread_start(sp3, p)
    scatter_send(rs_o)
    reduce_steps(2)
    spread_near(sp3)

    def attend_back(y, at, h, first):
        g = gatt[at, h * HEAD_DIM : (h + 1) * HEAD_DIM]
        o = att[at, h * HEAD_DIM : (h + 1) * HEAD_DIM]
        probs = pbuf[h, at, :]
        dv = tn(probs.astype(BF), g)
        dprobs = nt(g, value(h))
        delta = jnp.sum(g.astype(F32) * o.astype(F32), axis=-1, keepdims=True)
        ds = (probs * (dprobs - delta) * scale).astype(BF)
        dqs[h, at, :] = nn(ds, key(h))
        dk = tn(ds, query(h, at))
        if first:
            dvs[h] = dv
            dks[h] = dk
        else:
            dvs[h] += dv
            dks[h] += dk

    gatt[near, :] = nn(pair_of(x3, ypos), wof[...]).astype(BF)
    for h in range(heads):
        attend_back(ypos, near, h, True)
    for p in range(PARTS):
        spread_forward(sp3, p)
    reduce_steps(4)
    spread_far(sp3)
    gatt[far, :] = nn(pair_of(x3, 1 - ypos), wof[...]).astype(BF)
    g_heads = []
    for h in range(heads):
        attend_back(1 - ypos, far, h, False)
        t = slice(h * 128, (h + 1) * 128)

        @pl.loop(0, nmp)
        def _(r):
            at = chunk(r)
            u = jnp.concatenate([dqs[h, at, :], dks[h, at, :]], axis=1)
            pg[at, t] = (u * cos_t[at, :] - swap_halves(u) * sin_t[at, :]).astype(BF)

        g_h = grad_open(one, h * 128, (h + 1) * 128)
        gs1[:, :, t] = product(xt1, 1 - zb, pg[:, t]).astype(BF)
        grad_start(g_h)
        gw1[:, :, t] = product(xt1, zb, pg[:, t])
        g_heads.append(g_h)
        reduce_steps(2)

    pg[:, 2 * lw :] = jnp.concatenate([dvs[h] for h in range(heads)], axis=1).astype(BF)
    qkv_flat = wf1[:, :, : 3 * lw].reshape(width, 3 * lw)
    rs_f = scatter_open(2)
    scatter_far(rs_f, pg, qkv_flat)
    turn(x3, xt3)
    g_vo = grad_open(one, 2 * lw, 4 * lw)
    gs1[:, :, 2 * lw :] = jnp.concatenate(
        [product(xt1, 1 - zb, pg[:, 2 * lw :]), product(xt3, 1 - zb, att[...])], axis=2
    ).astype(BF)
    grad_start(g_vo)
    scatter_send(rs_f)
    gw1[:, :, 2 * lw :] = jnp.concatenate(
        [product(xt1, zb, pg[:, 2 * lw :]), product(xt3, zb, att[...])], axis=2
    )
    scatter_near(rs_f, pg, qkv_flat)
    reduce_steps(99)
    for g_h in g_heads:
        for k in (2, 1, 3):
            grad_middle(g_h, k)

    for p in range(PARTS):
        at = part_at(p)
        out_o[at, :] = mixed[at, :] + scatter_end(rs_o, p)
    total_two = jnp.concatenate([grad_end(g) for g in g_two], axis=1)
    for i in range(2):
        di_o[:, i, :] = total_two[:, i * units : (i + 1) * units]
    sum_two = jnp.sum(
        total_two[:, : 2 * units] * w2[:, : 2 * units].astype(F32), axis=-1, keepdims=True
    )
    dd_o[...] = flip(total_two[:, 2 * units : 3 * units])
    for p in range(PARTS):
        at = part_at(p)
        own_inv = inv_one[p * part_rows : (p + 1) * part_rows]
        back_one = norm_back(scatter_end(rs_f, p), xh1[at, :], own_inv, gain_one)
        tg_o[at, :] = mgrad[at, :] + back_one
    for k in (2, 1, 3):
        grad_middle(g_vo, k)
    qk_total = [grad_end(g_h) for g_h in g_heads]
    vo_total = grad_end(g_vo)
    sum_one = jnp.sum(
        vo_total[:, :lw] * w1[:, 2 * lw : 3 * lw].astype(F32), axis=-1, keepdims=True
    )
    for h in range(heads):
        sum_one += jnp.sum(
            qk_total[h] * w1[:, h * 128 : (h + 1) * 128].astype(F32), axis=-1, keepdims=True
        )
    lane = lax.broadcasted_iota(jnp.int32, (shard, 128), 1)
    sums = jnp.where(lane < 1, sum_one / column(gain_a), sum_two / column(gain_b))
    ggs[...] = flip(sums)[:8]
    gain_sems = [slot() for _ in range(3)]
    for k, other in enumerate((ypeer, mate, diag)):
        put(ggs, ggr.at[k], gain_sems[k], at_mp(other))
    dq_o[0] = jnp.concatenate([t[:, :HEAD_DIM] for t in qk_total], axis=1)
    dq_o[1] = jnp.concatenate([t[:, HEAD_DIM:] for t in qk_total], axis=1)
    dq_o[2] = vo_total[:, :lw]
    do_o[...] = flip(vo_total[:, lw:])
    total = ggs[...]
    for k in range(3):
        got(ggr.at[k], gain_sems[k])
        total = total + ggr[k]
    ga_o[...] = total[0:1]
    gb_o[...] = total[1:2]
    for copy in sends:
        copy.wait_send()


def settle_kernel(*refs):
    count = (len(refs) - 1) // 2
    sems = refs[-1]
    copies = [
        pltpu.make_async_copy(src, dst, sems.at[i])
        for i, (src, dst) in enumerate(zip(refs[:count], refs[count:-1]))
    ]
    for copy in copies:
        copy.start()
    for copy in copies:
        copy.wait()


def fused_shards(tokens, cotangent, attn_gain, w_qkv, w_attn_out, mlp_gain, w_in, w_mlp_out):
    ndp = lax.axis_size("dp")
    nmp = lax.axis_size("mp")
    rows, width = tokens.shape
    shard = w_qkv.shape[0]
    lw = w_qkv.shape[2]
    units = w_in.shape[2]
    heads = lw // HEAD_DIM
    length = rows * nmp
    na = ndp // PAIR
    half = HEAD_DIM // 2
    cols_one = 4 * lw
    cols_two = -(-3 * units // 128) * 128
    freqs = rope_base ** (-(np.arange(half, dtype=np.float32) * np.float32(2.0) / HEAD_DIM))
    angles = np.arange(length, dtype=np.float32)[:, None] * freqs.astype(np.float32)[None, :]
    cos_t = np.tile(np.cos(angles).astype(np.float32), (1, 128 // half))
    sin = np.sin(angles).astype(np.float32)
    sin_t = np.tile(np.concatenate([-sin, sin], axis=1), (1, 128 // HEAD_DIM))

    def buf(shape, dtype=BF):
        return pltpu.VMEM(shape, dtype)

    def grad_bufs(cols):
        return [
            buf((na, shard, cols)), buf((na, shard, cols)), buf((na, shard, cols)),
            buf((na, shard, cols)), buf((na, shard, cols), F32),
        ]

    nsem = ndp + 2 * na * (cols_one + cols_two) // 128 + 4 * (3 * PARTS) + 4 * (2 * PARTS + 1) + 2 * na * (4 + cols_two // 128) + 8
    scratch = [
        buf((3, shard, lw)), buf((lw, shard)), buf((shard, 2, units)), buf((units, shard)),
        buf((length, 128), F32), buf((length, 128), F32),
        buf((8, 128), F32), buf((ndp, 8, 128), F32),
        buf((shard, cols_one)), buf((shard, cols_two)),
        buf((ndp, shard, cols_one)), buf((ndp, shard, cols_two)), buf((width, lw)),
        *[buf((nmp, rows, width)) for _ in range(5)],
        *[buf((na, PAIR, shard, length)) for _ in range(4)],
        buf((length, heads * 128)), buf((length, lw)), buf((length, lw)),
        buf((heads, length, length), F32), buf((length, units)),
        buf((length, max(3 * lw, 2 * units)), F32), buf((length, units), F32),
        buf((length, 2 * units)), buf((length, 3 * lw)), buf((length, lw)),
        *[buf((heads, length, HEAD_DIM), F32) for _ in range(3)],
        *[buf((rows, width), F32) for _ in range(4)],
        buf((4, 2, rows, width)), buf((4, 2, rows, width)),
        buf((4, rows, width)), buf((4, rows, width)), buf((4, 2, rows, width), F32),
        *grad_bufs(cols_one), *grad_bufs(cols_two),
        buf((8, shard), F32), buf((3, 8, shard), F32),
        pltpu.SemaphoreType.DMA((nsem,)), pltpu.SemaphoreType.DMA((nsem,)),
        pltpu.SemaphoreType.DMA((8,)),
    ]
    vmem = pl.BlockSpec(memory_space=pltpu.VMEM)
    hbm = pl.BlockSpec(memory_space=pl.ANY)
    shapes = [
        (rows, width), (rows, width), (1, shard), (1, shard), (3, shard, lw), (lw, shard),
        (shard, 2, units), (units, shard),
    ]
    results = pl.pallas_call(
        functools.partial(layer_kernel, ndp, heads),
        out_shape=[buf(s, F32) for s in shapes],
        in_specs=[hbm, hbm, vmem, vmem, hbm, hbm, hbm, hbm, hbm, hbm],
        out_specs=[vmem] * 8,
        scratch_shapes=scratch,
        compiler_params=pltpu.CompilerParams(
            collective_id=0, has_side_effects=True, vmem_limit_bytes=56 * 1024 * 1024
        ),
    )(
        tokens, cotangent, attn_gain.reshape(1, shard), mlp_gain.reshape(1, shard),
        w_qkv.transpose(1, 0, 2), w_attn_out, w_in, w_mlp_out,
        jnp.asarray(cos_t), jnp.asarray(sin_t),
    )
    out, tg, ga, gb, dq, do, di, dd = pl.pallas_call(
        settle_kernel,
        out_shape=[jax.ShapeDtypeStruct(s, F32) for s in shapes],
        in_specs=[vmem] * 8,
        out_specs=[hbm] * 8,
        scratch_shapes=[pltpu.SemaphoreType.DMA((8,))],
    )(*[pltpu.with_memory_space_constraint(r, pltpu.VMEM) for r in results])
    return (
        out, tg, ga.reshape(shard), dq.transpose(1, 0, 2), do, gb.reshape(shard), di, dd,
    )


def choose(tokens, cotangent, attn_gain, w_qkv, w_attn_out, mlp_gain, w_in, w_mlp_out):
    ndp = lax.axis_size("dp")
    shard = w_qkv.shape[0]
    fits = (
        lax.axis_size("mp") == 4
        and ndp % PAIR == 0
        and shard % 16 == 0
        and shard <= 128
        and w_mlp_out.shape[1] == shard
        and tokens.shape[0] % 128 == 0
        and tokens.shape[0] <= 128
        and 4 * w_qkv.shape[2] % 128 == 0
        and w_qkv.shape[2] % HEAD_DIM == 0
    )
    form = fused_shards if fits else shards
    return form(tokens, cotangent, attn_gain, w_qkv, w_attn_out, mlp_gain, w_in, w_mlp_out)


def solution(mesh):
    in_specs = (
        P(("dp", "mp"), None),
        P(("dp", "mp"), None),
        P("dp"),
        P("dp", None, "mp"),
        P("mp", "dp"),
        P("dp"),
        P("dp", None, "mp"),
        P("mp", "dp"),
    )
    out_specs = (
        P(("dp", "mp"), None),
        P(("dp", "mp"), None),
        P("dp"),
        P("dp", None, "mp"),
        P("mp", "dp"),
        P("dp"),
        P("dp", None, "mp"),
        P("mp", "dp"),
    )
    return jax.shard_map(choose, mesh=mesh, in_specs=in_specs, out_specs=out_specs, check_vma=False)
```

```python
import functools

import jax
import jax.numpy as jnp
import numpy as np
from jax import lax
from jax.experimental import pallas as pl
from jax.experimental.pallas import tpu as pltpu
from jax.sharding import PartitionSpec as P

MESH = pl.DeviceIdType.MESH
PAIR = 2
PARTS = 2
AHEAD = 2
BF = jnp.bfloat16
F32 = jnp.float32

HEAD_DIM = 64


norm_eps = 1e-05
rope_base = 160000.0
query_block = 512


def rotary_tables(length, head_width):
    half_width = head_width // 2
    freqs = rope_base ** (-(jnp.arange(half_width, dtype=jnp.float32) * 2.0 / head_width))
    angles = jnp.arange(length, dtype=jnp.float32)[:, None] * freqs[None, :]
    angles = jnp.concatenate([angles, angles], axis=1)
    return (jnp.cos(angles), jnp.sin(angles))


def rotate_half(values):
    half_width = values.shape[-1] // 2
    return jnp.concatenate([-values[..., half_width:], values[..., :half_width]], axis=-1)


def apply_rotary(values, cosine_table, sine_table):
    return values * cosine_table[:, None, :] + rotate_half(values) * sine_table[:, None, :]


def undo_rotary(grads, cosine_table, sine_table):
    return grads * cosine_table[:, None, :] - rotate_half(grads * sine_table[:, None, :])


def norm_stats(values):
    centered = values - jnp.mean(values, axis=-1, keepdims=True)
    variance = jnp.mean(centered * centered, axis=-1, keepdims=True)
    inverse = lax.rsqrt(variance + norm_eps)
    return (centered * inverse, inverse)


def norm_backward(grad_out, normed, inverse, gain_vals):
    scaled = grad_out * gain_vals
    grad_in = inverse * (
        scaled
        - jnp.mean(scaled, axis=-1, keepdims=True)
        - normed * jnp.mean(scaled * normed, axis=-1, keepdims=True)
    )
    return (grad_in, jnp.sum(grad_out * normed, axis=0))


def gelu_exact(values):
    return 0.5 * values * (1.0 + jax.scipy.special.erf(values * 0.7071067811865476))


def gelu_slope(values):
    return (
        0.5 * (1.0 + jax.scipy.special.erf(values * 0.7071067811865476))
        + values * jnp.exp(-0.5 * values * values) * 0.3989422804014327
    )


def contract_rows(left, right):
    return lax.dot_general(
        left, right, (((0,), (0,)), ((), ())), preferred_element_type=jnp.float32
    )


def times_transposed(left, right):
    return lax.dot_general(
        left, right, (((1,), (1,)), ((), ())), preferred_element_type=jnp.float32
    )


def attention_weights(attn_gain, w_qkv, w_attn_out):
    return (
        lax.all_gather(attn_gain, "dp", axis=0, tiled=True),
        lax.all_gather(w_qkv, "dp", axis=0, tiled=True),
        lax.all_gather(w_attn_out, "dp", axis=1, tiled=True),
    )


def feedforward_weights(mlp_gain, w_in, w_mlp_out):
    return (
        lax.all_gather(mlp_gain, "dp", axis=0, tiled=True),
        lax.all_gather(w_in, "dp", axis=0, tiled=True),
        lax.all_gather(w_mlp_out, "dp", axis=1, tiled=True),
    )


def attention_forward(queries, key_rows, value_rows):
    length, head_count, head_width = queries.shape
    block_size = min(query_block, length)
    score_scale = head_width ** (-0.5)
    blocks = queries.reshape(length // block_size, block_size, head_count, head_width)

    def one_block(block_rows):
        scores = (
            jnp.einsum("qhd,khd->hqk", block_rows, key_rows, preferred_element_type=jnp.float32)
            * score_scale
        )
        row_peak = jnp.max(scores, axis=-1, keepdims=True)
        exp_scores = jnp.exp(scores - row_peak)
        row_total = jnp.sum(exp_scores, axis=-1, keepdims=True)
        attn_probs = (exp_scores / row_total).astype(jnp.bfloat16)
        block_out = jnp.einsum(
            "hqk,khd->qhd", attn_probs, value_rows, preferred_element_type=jnp.float32
        )
        return (block_out.astype(jnp.bfloat16), (row_peak + jnp.log(row_total))[..., 0])

    outs, log_totals = lax.map(one_block, blocks)
    return (outs.reshape(length, head_count, head_width), log_totals)


def attention_backward(queries, key_rows, value_rows, attended, log_totals, grad_out):
    length, head_count, head_width = queries.shape
    block_size = min(query_block, length)
    nblocks = length // block_size
    score_scale = head_width ** (-0.5)

    def one_block(running, block_inputs):
        key_grad, value_grad = running
        block_rows, out_rows, grad_rows, lse_rows = block_inputs
        scores = (
            jnp.einsum("qhd,khd->hqk", block_rows, key_rows, preferred_element_type=jnp.float32)
            * score_scale
        )
        attn_probs = jnp.exp(scores - lse_rows[..., None])
        value_grad = value_grad + jnp.einsum(
            "hqk,qhd->khd",
            attn_probs.astype(jnp.bfloat16),
            grad_rows,
            preferred_element_type=jnp.float32,
        )
        dprobs = jnp.einsum(
            "qhd,khd->hqk", grad_rows, value_rows, preferred_element_type=jnp.float32
        )
        row_delta = jnp.sum(grad_rows.astype(jnp.float32) * out_rows.astype(jnp.float32), axis=-1).T
        dscores = (attn_probs * (dprobs - row_delta[..., None]) * score_scale).astype(jnp.bfloat16)
        query_grad = jnp.einsum(
            "hqk,khd->qhd", dscores, key_rows, preferred_element_type=jnp.float32
        )
        key_grad = key_grad + jnp.einsum(
            "hqk,qhd->khd", dscores, block_rows, preferred_element_type=jnp.float32
        )
        return ((key_grad, value_grad), query_grad)

    zero_grad = jnp.zeros((length, head_count, head_width), jnp.float32)
    shape_blocks = (nblocks, block_size, head_count, head_width)
    block_inputs = (
        queries.reshape(shape_blocks),
        attended.reshape(shape_blocks),
        grad_out.reshape(shape_blocks),
        log_totals,
    )
    (key_grad, value_grad), query_grad = lax.scan(one_block, (zero_grad, zero_grad), block_inputs)
    return (query_grad.reshape(length, head_count, head_width), key_grad, value_grad)


def shards(tokens, cotangent, attn_gain, w_qkv, w_attn_out, mlp_gain, w_in, w_mlp_out):
    gain_one, qkv_full, out_full = attention_weights(attn_gain, w_qkv, w_attn_out)
    gain_two, in_full, down_full = feedforward_weights(mlp_gain, w_in, w_mlp_out)
    model_width = tokens.shape[1]
    residual = tokens.astype(jnp.float32)
    normed_one, inverse_one = norm_stats(residual)
    first_in = (normed_one * gain_one.astype(jnp.float32)).astype(jnp.bfloat16)
    first_all = lax.all_gather(first_in, "mp", axis=0, tiled=True)
    length = first_all.shape[0]
    local_width = qkv_full.shape[2]
    head_count = local_width // HEAD_DIM
    cosine_table, sine_table = rotary_tables(length, HEAD_DIM)
    projected = jnp.dot(
        first_all,
        qkv_full.reshape(model_width, 3 * local_width),
        preferred_element_type=jnp.float32,
    )
    projected = projected.reshape(length, 3, head_count, HEAD_DIM)
    queries = apply_rotary(projected[:, 0], cosine_table, sine_table).astype(jnp.bfloat16)
    key_rows = apply_rotary(projected[:, 1], cosine_table, sine_table).astype(jnp.bfloat16)
    value_rows = projected[:, 2].astype(jnp.bfloat16)
    attended, log_totals = attention_forward(queries, key_rows, value_rows)
    attended_flat = attended.reshape(length, local_width)
    mixed_rows = residual + lax.psum_scatter(
        jnp.dot(attended_flat, out_full, preferred_element_type=jnp.float32),
        "mp",
        scatter_dimension=0,
        tiled=True,
    )
    normed_two, inverse_two = norm_stats(mixed_rows)
    second_in = (normed_two * gain_two.astype(jnp.float32)).astype(jnp.bfloat16)
    second_all = lax.all_gather(second_in, "mp", axis=0, tiled=True)
    unit_count = in_full.shape[2]
    lifted = jnp.dot(
        second_all, in_full.reshape(model_width, 2 * unit_count), preferred_element_type=jnp.float32
    )
    lifted = lifted.reshape(length, 2, unit_count)
    inputs = lifted[:, 0]
    gate_vals = lifted[:, 1]
    activated = gelu_exact(inputs)
    hidden = (activated * gate_vals).astype(jnp.bfloat16)
    output = mixed_rows + lax.psum_scatter(
        jnp.dot(hidden, down_full, preferred_element_type=jnp.float32).astype(jnp.bfloat16),
        "mp",
        scatter_dimension=0,
        tiled=True,
    ).astype(jnp.float32)
    gain_two, in_full, down_full = feedforward_weights(mlp_gain, w_in, w_mlp_out)
    gain_one, qkv_full, out_full = attention_weights(attn_gain, w_qkv, w_attn_out)
    cot_all = lax.all_gather(cotangent, "mp", axis=0, tiled=True)
    hidden_grad = times_transposed(cot_all, down_full)
    down_grad = contract_rows(hidden, cot_all)
    input_grad = hidden_grad * gate_vals * gelu_slope(inputs)
    gate_grad = hidden_grad * activated
    lifted_grad = (
        jnp.stack([input_grad, gate_grad], axis=1)
        .astype(jnp.bfloat16)
        .reshape(length, 2 * unit_count)
    )
    in_grad = contract_rows(second_all, lifted_grad).reshape(model_width, 2, unit_count)
    in_flat = in_full.reshape(model_width, 2 * unit_count)
    second_grad = lax.psum_scatter(
        times_transposed(lifted_grad, in_flat), "mp", scatter_dimension=0, tiled=True
    )
    back_two, gain_two_part = norm_backward(
        second_grad, normed_two, inverse_two, gain_two.astype(jnp.float32)
    )
    mixed_grad = cotangent.astype(jnp.float32) + back_two
    mixed_low = mixed_grad.astype(jnp.bfloat16)
    mixed_all = lax.all_gather(mixed_low, "mp", axis=0, tiled=True)
    attended_grad = (
        times_transposed(mixed_all, out_full)
        .astype(jnp.bfloat16)
        .reshape(length, head_count, HEAD_DIM)
    )
    out_grad = contract_rows(attended_flat, mixed_all)
    query_grad, key_grad, value_grad = attention_backward(
        queries, key_rows, value_rows, attended, log_totals, attended_grad
    )
    query_grad = undo_rotary(query_grad, cosine_table, sine_table)
    key_grad = undo_rotary(key_grad, cosine_table, sine_table)
    projected_grad = (
        jnp.stack([query_grad, key_grad, value_grad], axis=1)
        .astype(jnp.bfloat16)
        .reshape(length, 3 * local_width)
    )
    qkv_grad = contract_rows(first_all, projected_grad).reshape(model_width, 3, local_width)
    qkv_flat = qkv_full.reshape(model_width, 3 * local_width)
    first_grad = lax.psum_scatter(
        times_transposed(projected_grad, qkv_flat).astype(jnp.bfloat16),
        "mp",
        scatter_dimension=0,
        tiled=True,
    ).astype(jnp.float32)
    back_one, gain_one_part = norm_backward(
        first_grad, normed_one, inverse_one, gain_one.astype(jnp.float32)
    )
    tokens_grad = mixed_grad + back_one
    down_shard, in_shard, gain_two_shard, out_shard, qkv_shard, gain_one_shard = (
        lax.psum_scatter(down_grad, "dp", scatter_dimension=1, tiled=True),
        lax.psum_scatter(in_grad, "dp", scatter_dimension=0, tiled=True),
        lax.psum_scatter(gain_two_part, "dp", scatter_dimension=0, tiled=True),
        lax.psum_scatter(out_grad, "dp", scatter_dimension=1, tiled=True),
        lax.psum_scatter(qkv_grad, "dp", scatter_dimension=0, tiled=True),
        lax.psum_scatter(gain_one_part, "dp", scatter_dimension=0, tiled=True),
    )
    gain_one_grad, gain_two_grad = lax.psum((gain_one_shard, gain_two_shard), "mp")
    return (
        output,
        tokens_grad,
        gain_one_grad,
        qkv_shard,
        out_shard,
        gain_two_grad,
        in_shard,
        down_shard,
    )


def nn(left, right):
    return lax.dot_general(left, right, (((1,), (0,)), ((), ())), preferred_element_type=F32)


def nt(left, right):
    return lax.dot_general(left, right, (((1,), (1,)), ((), ())), preferred_element_type=F32)


def tn(left, right):
    return lax.dot_general(left, right, (((0,), (0,)), ((), ())), preferred_element_type=F32)


def erf(x):
    return lax.erf(x)


def swap_halves(tile):
    lane = lax.broadcasted_iota(jnp.int32, tile.shape, 1)
    half = HEAD_DIM // 2
    back = pltpu.roll(tile, tile.shape[1] - half, 1)
    ahead = pltpu.roll(tile, half, 1)
    return jnp.where(lax.rem(lane, HEAD_DIM) < half, back, ahead)


def layer_kernel(
    ndp, heads,
    tok_h, cot_h, gain_a, gain_b, wq_h, wo_h, wi_h, wd_h, cos_h, sin_h,
    out_o, tg_o, ga_o, gb_o, dq_o, do_o, di_o, dd_o,
    wq_in, wo_in, wi_in, wd_in, cos_t, sin_t,
    gpad, gains, w1, w2, wf1, wf2, wof,
    xr, x1, x2, xc, x3, xt1, xt2, xtc, xt3,
    qk, vb, att, pbuf, hid, wide, hgrad_buf, lg, pg, gatt, dqs, dks, dvs,
    xh1, xh2, mixed, mgrad,
    rs_sc, rs_rc, rs_sy, rs_ry, rs_own,
    gs1, gr1, gz1, gy1, gw1,
    gs2, gr2, gz2, gy2, gw2,
    gv, gvr, ggs, ggr,
    send_sem, recv_sem, load_sem,
):
    nmp, rows, width = xr.shape
    length = nmp * rows
    na = ndp // PAIR
    dp = lax.axis_index("dp")
    mp = lax.axis_index("mp")
    za = dp // PAIR
    zb = lax.rem(dp, PAIR)
    core = lax.rem(mp, 2)
    ypos = mp // 2
    mate = mp + 1 - 2 * core
    ypeer = mp + 2 - 4 * ypos
    diag = mate + 2 - 4 * ypos
    xpeer = za * PAIR + (1 - zb)
    lw = heads * HEAD_DIM
    units = hid.shape[1]
    shard = w1.shape[0]
    cols_one, cols_two = w1.shape[1], w2.shape[1]

    def at_dp(d):
        return {"dp": d, "mp": mp}

    def at_mp(m):
        return {"dp": dp, "mp": m}

    counter = [0]
    sends = []

    def slot():
        counter[0] += 1
        return counter[0] - 1

    def put(src, dst, sem, dev):
        copy = pltpu.make_async_remote_copy(
            src_ref=src, dst_ref=dst, send_sem=send_sem.at[sem], recv_sem=recv_sem.at[sem],
            device_id=dev, device_id_type=MESH,
        )
        copy.start()
        sends.append(copy)

    def got(buf, sem):
        pltpu.make_async_remote_copy(
            src_ref=buf, dst_ref=buf, send_sem=send_sem.at[sem], recv_sem=recv_sem.at[sem],
            device_id=at_mp(mate), device_id_type=MESH,
        ).wait_recv()

    barrier = pltpu.get_barrier_semaphore()
    for k in range(1, ndp):
        pl.semaphore_signal(barrier, inc=1, device_id=at_dp(lax.rem(dp + k, ndp)), device_id_type=MESH)
    for other in (mate, ypeer, diag):
        pl.semaphore_signal(barrier, inc=1, device_id=at_mp(other), device_id_type=MESH)

    loads = [
        pltpu.make_async_copy(src, dst, load_sem.at[i])
        for i, (src, dst) in enumerate((
            (wq_h, wq_in), (tok_h, xr.at[mp]), (wo_h, wo_in), (wi_h, wi_in), (wd_h, wd_in),
            (cot_h, xc.at[mp]), (cos_h, cos_t), (sin_h, sin_t),
        ))
    ]
    for load in loads:
        load.start()

    def norm(vals):
        centered = vals - jnp.mean(vals, axis=-1, keepdims=True)
        inv = lax.rsqrt(jnp.mean(centered * centered, axis=-1, keepdims=True) + norm_eps)
        return centered * inv, inv

    def norm_back(grad, normed, inv, gain):
        scaled = grad * gain
        return inv * (
            scaled
            - jnp.mean(scaled, axis=-1, keepdims=True)
            - normed * jnp.mean(scaled * normed, axis=-1, keepdims=True)
        )

    def flip(vals):
        high, wide = vals.shape
        more_rows, more_cols = -high % 128, -wide % 128
        if more_cols:
            vals = jnp.concatenate([vals, jnp.zeros((high, more_cols), F32)], axis=1)
        if more_rows:
            vals = jnp.concatenate([vals, jnp.zeros((more_rows, wide + more_cols), F32)], axis=0)
        return vals.T[:wide, :high]

    def packed(q, k, v, o):
        parts = []
        for h in range(heads):
            parts += [q[:, h * HEAD_DIM : (h + 1) * HEAD_DIM], k[:, h * HEAD_DIM : (h + 1) * HEAD_DIM]]
        return jnp.concatenate([*parts, v, o], axis=1)

    gpad[...] = jnp.concatenate(
        [
            jnp.concatenate([gain_a[...].astype(F32), gain_b[...].astype(F32), jnp.zeros((6, shard), F32)], axis=0),
            jnp.zeros((8, 128 - shard), F32),
        ],
        axis=1,
    )
    loads[0].wait()
    loads[2].wait()
    w1[...] = packed(
        wq_in[0].astype(F32), wq_in[1].astype(F32), wq_in[2].astype(F32), flip(wo_in[...].astype(F32))
    ).astype(BF)
    loads[3].wait()
    loads[4].wait()
    w2[...] = jnp.concatenate(
        [
            wi_in[:, 0, :].astype(F32), wi_in[:, 1, :].astype(F32), flip(wd_in[...].astype(F32)),
            jnp.zeros((shard, cols_two - 3 * units), F32),
        ],
        axis=1,
    ).astype(BF)
    loads[1].wait()
    loads[5].wait()
    loads[6].wait()
    loads[7].wait()
    pl.semaphore_wait(barrier, ndp - 1 + 3)

    def gather_open(src, full, lo, hi):
        at = pl.ds(lo, hi - lo)
        return (src, full, at, [slot() for _ in range(na)], [slot() for _ in range(na)])

    def gather_far(state):
        src, full, at, zs, xs = state
        for k in (2, 1, 3):
            put(src.at[:, at], full.at[dp, :, at], zs[k], at_dp(lax.rem(za + k, na) * PAIR + zb))

    def gather_near(state):
        src, full, at, zs, xs = state
        put(src.at[:, at], full.at[dp, :, at], xs[0], at_dp(xpeer))

    def gather_forward(state, k):
        src, full, at, zs, xs = state
        source = lax.rem(za + na - k, na) * PAIR + zb
        got(full.at[source, :, at], zs[k])
        put(full.at[source, :, at], full.at[source, :, at], xs[k], at_dp(xpeer))

    def gather_end(state):
        src, full, at, zs, xs = state
        for k in range(na):
            source = lax.rem(za + na - k, na) * PAIR + (1 - zb)
            got(full.at[source, :, at], xs[k])

    order = (1, 3, 2)
    part_rows = rows // PARTS

    def part_at(p):
        return pl.ds(p * part_rows, part_rows)

    def spread_open(buf):
        return (buf, [[slot() for _ in range(3)] for _ in range(PARTS)])

    def spread_start(state, p):
        buf, sems = state
        block = buf.at[mp, part_at(p)]
        put(block, block, sems[p][0], at_mp(ypeer))
        put(block, block, sems[p][1], at_mp(mate))

    def spread_near(state):
        buf, sems = state
        for p in range(PARTS):
            got(buf.at[mate, part_at(p)], sems[p][1])

    def spread_forward(state, p):
        buf, sems = state
        block = buf.at[ypeer, part_at(p)]
        got(block, sems[p][0])
        put(block, block, sems[p][2], at_mp(mate))

    def spread_far(state):
        buf, sems = state
        for p in range(PARTS):
            got(buf.at[diag, part_at(p)], sems[p][2])

    def chunk(r):
        return pl.ds(pl.multiple_of(r * rows, rows), rows)

    def pair_rows(y):
        return pl.ds(pl.multiple_of(y * 2 * rows, 2 * rows), 2 * rows)

    near, far = pair_rows(ypos), pair_rows(1 - ypos)

    def pair_of(buf, y):
        return buf[pl.ds(pl.multiple_of(y * 2, 2), 2)].reshape(2 * rows, width)

    def scatter_open(i):
        return (i, [slot() for _ in range(PARTS)], slot(), [slot() for _ in range(PARTS)])

    def gain_part(part, x, r, row):
        if x is not None:
            gv[row : row + 1, :] += jnp.sum(part * x[r].astype(F32), axis=0, keepdims=True)

    def scatter_far(state, left, weights, x=None, row=0):
        i, s_far, s_near, s_y = state
        part = nt(left[chunk(diag), :], weights)
        rs_sc[i, 0] = part.astype(BF)
        for p in range(PARTS):
            at = part_at(p)
            put(rs_sc.at[i, 0, at], rs_rc.at[i, 0, at], s_far[p], at_mp(mate))
        gain_part(part, x, diag, row)
        part = nt(left[chunk(ypeer), :], weights)
        rs_own[i, 0] = part
        gain_part(part, x, ypeer, row)

    def scatter_send(state):
        i, s_far, s_near, s_y = state
        for p in range(PARTS):
            at = part_at(p)
            got(rs_rc.at[i, 0, at], s_far[p])
            rs_sy[i, at, :] = (rs_own[i, 0, at, :] + rs_rc[i, 0, at, :].astype(F32)).astype(BF)
            put(rs_sy.at[i, at], rs_ry.at[i, at], s_y[p], at_mp(ypeer))

    def scatter_near(state, left, weights, x=None, row=0):
        i, s_far, s_near, s_y = state
        part = nt(left[chunk(mate), :], weights)
        rs_sc[i, 1] = part.astype(BF)
        put(rs_sc.at[i, 1], rs_rc.at[i, 1], s_near, at_mp(mate))
        gain_part(part, x, mate, row)
        part = nt(left[chunk(mp), :], weights)
        rs_own[i, 1] = part
        gain_part(part, x, mp, row)

    def scatter_end(state, p):
        i, s_far, s_near, s_y = state
        at = part_at(p)
        if p == 0:
            got(rs_rc.at[i, 1], s_near)
        total = rs_own[i, 1, at, :] + rs_rc[i, 1, at, :].astype(F32)
        got(rs_ry.at[i, at], s_y[p])
        return total + rs_ry[i, at, :].astype(F32)

    def turn(buf, dst):
        @pl.loop(0, nmp)
        def _(r):
            cols = pl.ds(pl.multiple_of(r * rows, rows), rows)
            flipped = buf[r].T
            dst[:, :, :, cols] = flipped.reshape(na, PAIR, shard, rows)

    def product(xt, half, right):
        return nn(xt[:, half].reshape(na * shard, length), right).reshape(na, shard, right.shape[1])

    def grad_open(bufs, lo, hi):
        return (bufs, pl.ds(lo, hi - lo), [slot() for _ in range(na)], [slot() for _ in range(na)])

    def grad_start(state):
        (gs, gr, gz, gy, gw), at, xs, zs = state
        for k in (2, 1, 3, 0):
            a = lax.rem(za + k, na)
            put(gs.at[a, :, at], gr.at[a, :, at], xs[k], at_dp(xpeer))

    def grad_middle(state, k):
        (gs, gr, gz, gy, gw), at, xs, zs = state
        a = lax.rem(za + k, na)
        got(gr.at[a, :, at], xs[k])
        gz[k, :, at] = (gw[a, :, at] + gr[a, :, at].astype(F32)).astype(BF)
        put(gz.at[k, :, at], gy.at[k, :, at], zs[k], at_dp(a * PAIR + zb))

    def grad_end(state):
        (gs, gr, gz, gy, gw), at, xs, zs = state
        got(gr.at[za, :, at], xs[0])
        total = gw[za, :, at] + gr[za, :, at].astype(F32)
        for k in range(1, na):
            got(gy.at[k, :, at], zs[k])
            total = total + gy[k, :, at].astype(F32)
        return total

    one = (gs1, gr1, gz1, gy1, gw1)
    two = (gs2, gr2, gz2, gy2, gw2)

    gain_slots = [slot() for _ in range(ndp - 1)]
    for k in range(1, ndp):
        put(gpad, gains.at[dp], gain_slots[k - 1], at_dp(lax.rem(dp + k, ndp)))
    pieces = [gather_open(w1, wf1, c, c + 128) for c in range(0, cols_one, 128)]
    count_one = len(pieces)
    count_q = -(-3 * lw // 128)
    pieces += [gather_open(w2, wf2, c, c + 128) for c in range(0, cols_two, 128)]
    at_piece = [0]

    def pump(count):
        for _ in range(count):
            i = at_piece[0]
            if i >= len(pieces):
                return
            at_piece[0] += 1
            if i + AHEAD < len(pieces) and i < count_q:
                gather_far(pieces[i + AHEAD])
            if i + 1 < len(pieces) and i < count_q:
                gather_near(pieces[i + 1])
            for k in order:
                gather_forward(pieces[i], k)

    sp1 = spread_open(xr)
    gather_near(pieces[0])
    for i in range(AHEAD):
        gather_far(pieces[i])
        if i == 0:
            for p in range(PARTS):
                spread_start(sp1, p)
    gains[dp] = gpad[...]
    wf1[dp] = w1[...]
    wf2[dp] = w2[...]
    for k in range(1, ndp):
        source = lax.rem(dp + ndp - k, ndp)
        got(gains.at[source], gain_slots[k - 1])

    def whole_gain(i):
        return jnp.concatenate([gains[d, i : i + 1, :shard] for d in range(ndp)], axis=1)

    gain_one = whole_gain(0)
    gain_two = whole_gain(1)

    normed_one, inv_one = norm(xr[mp].astype(F32))
    xh1[...] = normed_one
    x1[mp] = (normed_one * gain_one).astype(BF)

    def first_norm(r):
        x1[r] = (norm(xr[r].astype(F32))[0] * gain_one).astype(BF)

    pump(1)
    spread_near(sp1)
    first_norm(mate)
    spc = spread_open(xc)
    pump(1)
    for p in range(PARTS):
        spread_forward(sp1, p)
        spread_start(spc, p)
    first_norm(ypeer)
    pump(1)
    spread_far(sp1)
    first_norm(diag)
    turn(x1, xt1)
    pump(count_q - 2)
    for p in range(PARTS):
        spread_forward(spc, p)
    for piece in pieces[count_q + AHEAD :]:
        gather_far(piece)
    for piece in pieces[count_q + 1 :]:
        gather_near(piece)
    for i in range(count_q):
        gather_end(pieces[i])

    wide[:, : 3 * lw] = nn(
        x1[...].reshape(length, width), wf1[:, :, : 3 * lw].reshape(width, 3 * lw)
    )

    @pl.loop(0, nmp)
    def _(r):
        at = chunk(r)
        for h in range(heads):
            t = slice(h * 128, (h + 1) * 128)
            u = wide[at, t]
            qk[at, t] = (u * cos_t[at, :] + swap_halves(u) * sin_t[at, :]).astype(BF)
        vb[at, :] = wide[at, 2 * lw : 3 * lw].astype(BF)

    scale = HEAD_DIM ** (-0.5)

    def query(h, at=slice(None)):
        return qk[at, h * 128 : h * 128 + HEAD_DIM]

    def key(h, at=slice(None)):
        return qk[at, h * 128 + HEAD_DIM : (h + 1) * 128]

    def value(h, at=slice(None)):
        return vb[at, h * HEAD_DIM : (h + 1) * HEAD_DIM]

    def attend(at):
        outs = []
        for h in range(heads):
            scores = nt(query(h, at), key(h)) * scale
            peak = jnp.max(scores, axis=-1, keepdims=True)
            e = jnp.exp(scores - peak)
            probs = e / jnp.sum(e, axis=-1, keepdims=True)
            pbuf[h, at, :] = probs
            outs.append(nn(probs.astype(BF), value(h)))
        att[at, :] = jnp.concatenate(outs, axis=1).astype(BF)

    pump(1)
    attend(far)
    pump(1)
    for i in range(count_q, count_one):
        gather_end(pieces[i])
    wof[...] = wf1[:, :, 3 * lw :].reshape(width, lw)
    rs_a = scatter_open(0)
    scatter_far(rs_a, att, wof[...])
    scatter_send(rs_a)
    attend(near)
    scatter_near(rs_a, att, wof[...])
    pump(1)
    spread_near(spc)
    spread_far(spc)
    turn(xc, xtc)
    pump(2)

    inv_two = []
    sp2 = spread_open(x2)
    for p in range(PARTS):
        at = part_at(p)
        mixed[at, :] = xr[mp, at, :].astype(F32) + scatter_end(rs_a, p)
        normed_two, inv = norm(mixed[at, :])
        inv_two.append(inv)
        xh2[at, :] = normed_two
        x2[mp, at, :] = (normed_two * gain_two).astype(BF)
        spread_start(sp2, p)
    def gelu_part(y, at):
        wide[at, : 2 * units] = nn(
            pair_of(x2, y), wf2[:, :, : 2 * units].reshape(width, 2 * units)
        )
        hgrad_buf[at, :] = nn(
            pair_of(xc, y), wf2[:, :, 2 * units : 3 * units].reshape(width, units)
        )

        @pl.loop(0, 2)
        def _(r):
            now = chunk(2 * y + r)
            u = wide[now, :units]
            gate = wide[now, units : 2 * units]
            cdf = 0.5 * (1.0 + erf(u * 0.7071067811865476))
            act = u * cdf
            slope = cdf + u * jnp.exp(-0.5 * u * u) * 0.3989422804014327
            hid[now, :] = (act * gate).astype(BF)
            hgrad = hgrad_buf[now, :]
            lg[now, :] = jnp.concatenate([hgrad * gate * slope, hgrad * act], axis=1).astype(BF)

    pump(1)
    spread_near(sp2)
    pump(1)
    for p in range(PARTS):
        spread_forward(sp2, p)
    spread_far(sp2)
    turn(x2, xt2)
    pump(len(pieces))
    for piece in pieces[count_one:]:
        gather_end(piece)
    gelu_part(ypos, near)
    gelu_part(1 - ypos, far)
    in_flat = wf2[:, :, : 2 * units].reshape(width, 2 * units)
    rs_g = scatter_open(1)
    gv[...] = jnp.zeros_like(gv)
    scatter_far(rs_g, lg, in_flat, x2, 1)
    g_two = [grad_open(two, c, c + 128) for c in range(0, cols_two, 128)]
    early = 2 * units // 128
    steps = []

    def leave(state):
        grad_start(state)
        steps.extend((state, k) for k in (2, 1, 3))

    def reduce_steps(count):
        for _ in range(min(count, len(steps))):
            grad_middle(*steps.pop(0))

    gs2[:, :, : 2 * units] = product(xt2, 1 - zb, lg[...]).astype(BF)
    for g in g_two[:early]:
        leave(g)
    scatter_send(rs_g)
    gs2[:, :, 2 * units : 3 * units] = product(xtc, 1 - zb, hid[...]).astype(BF)
    gs2[:, :, 3 * units :] = jnp.zeros((na, shard, cols_two - 3 * units), BF)
    for g in g_two[early:]:
        leave(g)
    scatter_near(rs_g, lg, in_flat, x2, 1)
    gw2[:, :, : 2 * units] = product(xt2, zb, lg[...])
    gw2[:, :, 2 * units : 3 * units] = product(xtc, zb, hid[...])
    gw2[:, :, 3 * units :] = jnp.zeros((na, shard, cols_two - 3 * units), F32)
    down_flat = wf2[:, :, 2 * units : 3 * units].reshape(width, units)
    rs_o = scatter_open(3)
    scatter_far(rs_o, hid, down_flat)
    scatter_near(rs_o, hid, down_flat)
    reduce_steps(5)
    sp3 = spread_open(x3)
    for p in range(PARTS):
        at = part_at(p)
        back_two = norm_back(scatter_end(rs_g, p), xh2[at, :], inv_two[p], gain_two)
        mgrad[at, :] = xc[mp, at, :].astype(F32) + back_two
        x3[mp, at, :] = mgrad[at, :].astype(BF)
        spread_start(sp3, p)
    scatter_send(rs_o)
    reduce_steps(3)
    spread_near(sp3)

    def attend_back(y, at, h, first):
        g = gatt[at, h * HEAD_DIM : (h + 1) * HEAD_DIM]
        o = att[at, h * HEAD_DIM : (h + 1) * HEAD_DIM]
        probs = pbuf[h, at, :]
        dv = tn(probs.astype(BF), g)
        dprobs = nt(g, value(h))
        delta = jnp.sum(g.astype(F32) * o.astype(F32), axis=-1, keepdims=True)
        ds = (probs * (dprobs - delta) * scale).astype(BF)
        dqs[h, at, :] = nn(ds, key(h))
        dk = tn(ds, query(h, at))
        if first:
            dvs[h] = dv
            dks[h] = dk
        else:
            dvs[h] += dv
            dks[h] += dk

    gatt[near, :] = nn(pair_of(x3, ypos), wof[...]).astype(BF)
    for h in range(heads):
        attend_back(ypos, near, h, True)
    for p in range(PARTS):
        spread_forward(sp3, p)
    reduce_steps(5)
    spread_far(sp3)
    gatt[far, :] = nn(pair_of(x3, 1 - ypos), wof[...]).astype(BF)
    turn(x3, xt3)
    late = -(-3 * lw // 128) * 128
    gs1[:, :, 3 * lw :] = product(xt3, 1 - zb, att[...]).astype(BF)
    g_one = {c: grad_open(one, c, c + 128) for c in range(0, cols_one, 128)}
    for c in range(late, cols_one, 128):
        leave(g_one[c])
    gw1[:, :, 3 * lw :] = product(xt3, zb, att[...])
    done = 2 * lw
    for h in range(heads):
        attend_back(1 - ypos, far, h, False)
        t = slice(h * 128, (h + 1) * 128)
        v = slice(2 * lw + h * HEAD_DIM, 2 * lw + (h + 1) * HEAD_DIM)

        @pl.loop(0, nmp)
        def _(r):
            at = chunk(r)
            u = jnp.concatenate([dqs[h, at, :], dks[h, at, :]], axis=1)
            pg[at, t] = (u * cos_t[at, :] - swap_halves(u) * sin_t[at, :]).astype(BF)
            pg[at, v] = dvs[h, at, :].astype(BF)

        gs1[:, :, t] = product(xt1, 1 - zb, pg[:, t]).astype(BF)
        leave(g_one[h * 128])
        last = h == heads - 1
        end = late if last else (2 * lw + (h + 1) * HEAD_DIM) // 128 * 128
        if end > done:
            ready = slice(done, min(end, 3 * lw))
            gs1[:, :, ready] = product(xt1, 1 - zb, pg[:, ready]).astype(BF)
            for c in range(done, end, 128):
                leave(g_one[c])
            gw1[:, :, ready] = product(xt1, zb, pg[:, ready])
            done = end
        gw1[:, :, t] = product(xt1, zb, pg[:, t])
        reduce_steps(3)

    qkv_flat = wf1[:, :, : 3 * lw].reshape(width, 3 * lw)
    rs_f = scatter_open(2)
    scatter_far(rs_f, pg, qkv_flat, x1, 0)
    reduce_steps(3)
    scatter_send(rs_f)
    scatter_near(rs_f, pg, qkv_flat, x1, 0)
    gain_sems = [slot() for _ in range(3)]
    for k, other in enumerate((ypeer, mate, diag)):
        put(gv, gvr.at[k], gain_sems[k], at_mp(other))
    reduce_steps(99)
    gain_sum = gv[...]
    for k in range(3):
        got(gvr.at[k], gain_sems[k])
        gain_sum = gain_sum + gvr[k]
    empty = jnp.zeros((8, 128 - shard), F32)
    for d in range(ndp):
        ggs[d] = jnp.concatenate([gain_sum[:, d * shard : (d + 1) * shard], empty], axis=1)
    sum_sems = [slot() for _ in range(ndp)]
    for k in range(1, ndp):
        d = lax.rem(dp + k, ndp)
        put(ggs.at[d], ggr.at[k], sum_sems[k], at_dp(d))

    for p in range(PARTS):
        at = part_at(p)
        out_o[at, :] = mixed[at, :] + scatter_end(rs_o, p)
    total_two = jnp.concatenate([grad_end(g) for g in g_two], axis=1)
    for i in range(2):
        di_o[:, i, :] = total_two[:, i * units : (i + 1) * units]
    dd_o[...] = flip(total_two[:, 2 * units : 3 * units])
    for p in range(PARTS):
        at = part_at(p)
        own_inv = inv_one[p * part_rows : (p + 1) * part_rows]
        back_one = norm_back(scatter_end(rs_f, p), xh1[at, :], own_inv, gain_one)
        tg_o[at, :] = mgrad[at, :] + back_one
    one_total = {c: grad_end(g) for c, g in sorted(g_one.items())}
    qk_total = [one_total[h * 128] for h in range(heads)]
    vo_total = jnp.concatenate([one_total[c] for c in range(2 * lw, cols_one, 128)], axis=1)
    dq_o[0] = jnp.concatenate([t[:, :HEAD_DIM] for t in qk_total], axis=1)
    dq_o[1] = jnp.concatenate([t[:, HEAD_DIM:] for t in qk_total], axis=1)
    dq_o[2] = vo_total[:, :lw]
    do_o[...] = flip(vo_total[:, lw:])
    total = ggs[dp]
    for k in range(1, ndp):
        got(ggr.at[k], sum_sems[k])
        total = total + ggr[k]
    ga_o[...] = total[0:1, :shard] / gain_a[...].astype(F32)
    gb_o[...] = total[1:2, :shard] / gain_b[...].astype(F32)
    for copy in sends:
        copy.wait_send()


def settle_kernel(*refs):
    count = (len(refs) - 1) // 2
    sems = refs[-1]
    copies = [
        pltpu.make_async_copy(src, dst, sems.at[i])
        for i, (src, dst) in enumerate(zip(refs[:count], refs[count:-1]))
    ]
    for copy in copies:
        copy.start()
    for copy in copies:
        copy.wait()


def fused_shards(tokens, cotangent, attn_gain, w_qkv, w_attn_out, mlp_gain, w_in, w_mlp_out):
    ndp = lax.axis_size("dp")
    nmp = lax.axis_size("mp")
    rows, width = tokens.shape
    shard = w_qkv.shape[0]
    lw = w_qkv.shape[2]
    units = w_in.shape[2]
    heads = lw // HEAD_DIM
    length = rows * nmp
    na = ndp // PAIR
    half = HEAD_DIM // 2
    cols_one = 4 * lw
    cols_two = -(-3 * units // 128) * 128
    freqs = rope_base ** (-(np.arange(half, dtype=np.float32) * np.float32(2.0) / HEAD_DIM))
    angles = np.arange(length, dtype=np.float32)[:, None] * freqs.astype(np.float32)[None, :]
    cos_t = np.tile(np.cos(angles).astype(np.float32), (1, 128 // half))
    sin = np.sin(angles).astype(np.float32)
    sin_t = np.tile(np.concatenate([-sin, sin], axis=1), (1, 128 // HEAD_DIM))

    def buf(shape, dtype=BF):
        return pltpu.VMEM(shape, dtype)

    def grad_bufs(cols):
        return [
            buf((na, shard, cols)), buf((na, shard, cols)), buf((na, shard, cols)),
            buf((na, shard, cols)), buf((na, shard, cols), F32),
        ]

    nsem = 2 * ndp + 2 * na * (cols_one + cols_two) // 128 + 4 * (3 * PARTS) + 4 * (2 * PARTS + 1) + 2 * na * (cols_one + cols_two) // 128 + 8
    scratch = [
        buf((3, shard, lw)), buf((lw, shard)), buf((shard, 2, units)), buf((units, shard)),
        buf((length, 128), F32), buf((length, 128), F32),
        buf((8, 128), F32), buf((ndp, 8, 128), F32),
        buf((shard, cols_one)), buf((shard, cols_two)),
        buf((ndp, shard, cols_one)), buf((ndp, shard, cols_two)), buf((width, lw)),
        *[buf((nmp, rows, width)) for _ in range(5)],
        *[buf((na, PAIR, shard, length)) for _ in range(4)],
        buf((length, heads * 128)), buf((length, lw)), buf((length, lw)),
        buf((heads, length, length), F32), buf((length, units)),
        buf((length, max(3 * lw, 2 * units)), F32), buf((length, units), F32),
        buf((length, 2 * units)), buf((length, 3 * lw)), buf((length, lw)),
        *[buf((heads, length, HEAD_DIM), F32) for _ in range(3)],
        *[buf((rows, width), F32) for _ in range(4)],
        buf((4, 2, rows, width)), buf((4, 2, rows, width)),
        buf((4, rows, width)), buf((4, rows, width)), buf((4, 2, rows, width), F32),
        *grad_bufs(cols_one), *grad_bufs(cols_two),
        buf((8, width), F32), buf((3, 8, width), F32), buf((ndp, 8, 128), F32), buf((ndp, 8, 128), F32),
        pltpu.SemaphoreType.DMA((nsem,)), pltpu.SemaphoreType.DMA((nsem,)),
        pltpu.SemaphoreType.DMA((8,)),
    ]
    vmem = pl.BlockSpec(memory_space=pltpu.VMEM)
    hbm = pl.BlockSpec(memory_space=pl.ANY)
    shapes = [
        (rows, width), (rows, width), (1, shard), (1, shard), (3, shard, lw), (lw, shard),
        (shard, 2, units), (units, shard),
    ]
    results = pl.pallas_call(
        functools.partial(layer_kernel, ndp, heads),
        out_shape=[buf(s, F32) for s in shapes],
        in_specs=[hbm, hbm, vmem, vmem, hbm, hbm, hbm, hbm, hbm, hbm],
        out_specs=[vmem] * 8,
        scratch_shapes=scratch,
        compiler_params=pltpu.CompilerParams(
            collective_id=0, has_side_effects=True, vmem_limit_bytes=56 * 1024 * 1024
        ),
    )(
        tokens, cotangent, attn_gain.reshape(1, shard), mlp_gain.reshape(1, shard),
        w_qkv.transpose(1, 0, 2), w_attn_out, w_in, w_mlp_out,
        jnp.asarray(cos_t), jnp.asarray(sin_t),
    )
    out, tg, ga, gb, dq, do, di, dd = pl.pallas_call(
        settle_kernel,
        out_shape=[jax.ShapeDtypeStruct(s, F32) for s in shapes],
        in_specs=[vmem] * 8,
        out_specs=[hbm] * 8,
        scratch_shapes=[pltpu.SemaphoreType.DMA((8,))],
    )(*[pltpu.with_memory_space_constraint(r, pltpu.VMEM) for r in results])
    return (
        out, tg, ga.reshape(shard), dq.transpose(1, 0, 2), do, gb.reshape(shard), di, dd,
    )


def choose(tokens, cotangent, attn_gain, w_qkv, w_attn_out, mlp_gain, w_in, w_mlp_out):
    ndp = lax.axis_size("dp")
    shard = w_qkv.shape[0]
    fits = (
        lax.axis_size("mp") == 4
        and ndp % PAIR == 0
        and shard % 16 == 0
        and shard <= 128
        and w_mlp_out.shape[1] == shard
        and tokens.shape[0] % 128 == 0
        and tokens.shape[0] <= 128
        and 4 * w_qkv.shape[2] % 128 == 0
        and w_qkv.shape[2] % HEAD_DIM == 0
    )
    form = fused_shards if fits else shards
    return form(tokens, cotangent, attn_gain, w_qkv, w_attn_out, mlp_gain, w_in, w_mlp_out)


def solution(mesh):
    in_specs = (
        P(("dp", "mp"), None),
        P(("dp", "mp"), None),
        P("dp"),
        P("dp", None, "mp"),
        P("mp", "dp"),
        P("dp"),
        P("dp", None, "mp"),
        P("mp", "dp"),
    )
    out_specs = (
        P(("dp", "mp"), None),
        P(("dp", "mp"), None),
        P("dp"),
        P("dp", None, "mp"),
        P("mp", "dp"),
        P("dp"),
        P("dp", None, "mp"),
        P("mp", "dp"),
    )
    return jax.shard_map(choose, mesh=mesh, in_specs=in_specs, out_specs=out_specs, check_vma=False)
```

```python
import functools

import jax
import jax.numpy as jnp
import numpy as np
from jax import lax
from jax.experimental import pallas as pl
from jax.experimental.pallas import tpu as pltpu
from jax.sharding import PartitionSpec as P

MESH = pl.DeviceIdType.MESH
PAIR = 2
PARTS = 2
AHEAD = 2
WINDOW = 2
BF = jnp.bfloat16
F32 = jnp.float32

HEAD_DIM = 64


norm_eps = 1e-05
rope_base = 160000.0
query_block = 512


def rotary_tables(length, head_width):
    half_width = head_width // 2
    freqs = rope_base ** (-(jnp.arange(half_width, dtype=jnp.float32) * 2.0 / head_width))
    angles = jnp.arange(length, dtype=jnp.float32)[:, None] * freqs[None, :]
    angles = jnp.concatenate([angles, angles], axis=1)
    return (jnp.cos(angles), jnp.sin(angles))


def rotate_half(values):
    half_width = values.shape[-1] // 2
    return jnp.concatenate([-values[..., half_width:], values[..., :half_width]], axis=-1)


def apply_rotary(values, cosine_table, sine_table):
    return values * cosine_table[:, None, :] + rotate_half(values) * sine_table[:, None, :]


def undo_rotary(grads, cosine_table, sine_table):
    return grads * cosine_table[:, None, :] - rotate_half(grads * sine_table[:, None, :])


def norm_stats(values):
    centered = values - jnp.mean(values, axis=-1, keepdims=True)
    variance = jnp.mean(centered * centered, axis=-1, keepdims=True)
    inverse = lax.rsqrt(variance + norm_eps)
    return (centered * inverse, inverse)


def norm_backward(grad_out, normed, inverse, gain_vals):
    scaled = grad_out * gain_vals
    grad_in = inverse * (
        scaled
        - jnp.mean(scaled, axis=-1, keepdims=True)
        - normed * jnp.mean(scaled * normed, axis=-1, keepdims=True)
    )
    return (grad_in, jnp.sum(grad_out * normed, axis=0))


def gelu_exact(values):
    return 0.5 * values * (1.0 + jax.scipy.special.erf(values * 0.7071067811865476))


def gelu_slope(values):
    return (
        0.5 * (1.0 + jax.scipy.special.erf(values * 0.7071067811865476))
        + values * jnp.exp(-0.5 * values * values) * 0.3989422804014327
    )


def contract_rows(left, right):
    return lax.dot_general(
        left, right, (((0,), (0,)), ((), ())), preferred_element_type=jnp.float32
    )


def times_transposed(left, right):
    return lax.dot_general(
        left, right, (((1,), (1,)), ((), ())), preferred_element_type=jnp.float32
    )


def attention_weights(attn_gain, w_qkv, w_attn_out):
    return (
        lax.all_gather(attn_gain, "dp", axis=0, tiled=True),
        lax.all_gather(w_qkv, "dp", axis=0, tiled=True),
        lax.all_gather(w_attn_out, "dp", axis=1, tiled=True),
    )


def feedforward_weights(mlp_gain, w_in, w_mlp_out):
    return (
        lax.all_gather(mlp_gain, "dp", axis=0, tiled=True),
        lax.all_gather(w_in, "dp", axis=0, tiled=True),
        lax.all_gather(w_mlp_out, "dp", axis=1, tiled=True),
    )


def attention_forward(queries, key_rows, value_rows):
    length, head_count, head_width = queries.shape
    block_size = min(query_block, length)
    score_scale = head_width ** (-0.5)
    blocks = queries.reshape(length // block_size, block_size, head_count, head_width)

    def one_block(block_rows):
        scores = (
            jnp.einsum("qhd,khd->hqk", block_rows, key_rows, preferred_element_type=jnp.float32)
            * score_scale
        )
        row_peak = jnp.max(scores, axis=-1, keepdims=True)
        exp_scores = jnp.exp(scores - row_peak)
        row_total = jnp.sum(exp_scores, axis=-1, keepdims=True)
        attn_probs = (exp_scores / row_total).astype(jnp.bfloat16)
        block_out = jnp.einsum(
            "hqk,khd->qhd", attn_probs, value_rows, preferred_element_type=jnp.float32
        )
        return (block_out.astype(jnp.bfloat16), (row_peak + jnp.log(row_total))[..., 0])

    outs, log_totals = lax.map(one_block, blocks)
    return (outs.reshape(length, head_count, head_width), log_totals)


def attention_backward(queries, key_rows, value_rows, attended, log_totals, grad_out):
    length, head_count, head_width = queries.shape
    block_size = min(query_block, length)
    nblocks = length // block_size
    score_scale = head_width ** (-0.5)

    def one_block(running, block_inputs):
        key_grad, value_grad = running
        block_rows, out_rows, grad_rows, lse_rows = block_inputs
        scores = (
            jnp.einsum("qhd,khd->hqk", block_rows, key_rows, preferred_element_type=jnp.float32)
            * score_scale
        )
        attn_probs = jnp.exp(scores - lse_rows[..., None])
        value_grad = value_grad + jnp.einsum(
            "hqk,qhd->khd",
            attn_probs.astype(jnp.bfloat16),
            grad_rows,
            preferred_element_type=jnp.float32,
        )
        dprobs = jnp.einsum(
            "qhd,khd->hqk", grad_rows, value_rows, preferred_element_type=jnp.float32
        )
        row_delta = jnp.sum(grad_rows.astype(jnp.float32) * out_rows.astype(jnp.float32), axis=-1).T
        dscores = (attn_probs * (dprobs - row_delta[..., None]) * score_scale).astype(jnp.bfloat16)
        query_grad = jnp.einsum(
            "hqk,khd->qhd", dscores, key_rows, preferred_element_type=jnp.float32
        )
        key_grad = key_grad + jnp.einsum(
            "hqk,qhd->khd", dscores, block_rows, preferred_element_type=jnp.float32
        )
        return ((key_grad, value_grad), query_grad)

    zero_grad = jnp.zeros((length, head_count, head_width), jnp.float32)
    shape_blocks = (nblocks, block_size, head_count, head_width)
    block_inputs = (
        queries.reshape(shape_blocks),
        attended.reshape(shape_blocks),
        grad_out.reshape(shape_blocks),
        log_totals,
    )
    (key_grad, value_grad), query_grad = lax.scan(one_block, (zero_grad, zero_grad), block_inputs)
    return (query_grad.reshape(length, head_count, head_width), key_grad, value_grad)


def shards(tokens, cotangent, attn_gain, w_qkv, w_attn_out, mlp_gain, w_in, w_mlp_out):
    gain_one, qkv_full, out_full = attention_weights(attn_gain, w_qkv, w_attn_out)
    gain_two, in_full, down_full = feedforward_weights(mlp_gain, w_in, w_mlp_out)
    model_width = tokens.shape[1]
    residual = tokens.astype(jnp.float32)
    normed_one, inverse_one = norm_stats(residual)
    first_in = (normed_one * gain_one.astype(jnp.float32)).astype(jnp.bfloat16)
    first_all = lax.all_gather(first_in, "mp", axis=0, tiled=True)
    length = first_all.shape[0]
    local_width = qkv_full.shape[2]
    head_count = local_width // HEAD_DIM
    cosine_table, sine_table = rotary_tables(length, HEAD_DIM)
    projected = jnp.dot(
        first_all,
        qkv_full.reshape(model_width, 3 * local_width),
        preferred_element_type=jnp.float32,
    )
    projected = projected.reshape(length, 3, head_count, HEAD_DIM)
    queries = apply_rotary(projected[:, 0], cosine_table, sine_table).astype(jnp.bfloat16)
    key_rows = apply_rotary(projected[:, 1], cosine_table, sine_table).astype(jnp.bfloat16)
    value_rows = projected[:, 2].astype(jnp.bfloat16)
    attended, log_totals = attention_forward(queries, key_rows, value_rows)
    attended_flat = attended.reshape(length, local_width)
    mixed_rows = residual + lax.psum_scatter(
        jnp.dot(attended_flat, out_full, preferred_element_type=jnp.float32),
        "mp",
        scatter_dimension=0,
        tiled=True,
    )
    normed_two, inverse_two = norm_stats(mixed_rows)
    second_in = (normed_two * gain_two.astype(jnp.float32)).astype(jnp.bfloat16)
    second_all = lax.all_gather(second_in, "mp", axis=0, tiled=True)
    unit_count = in_full.shape[2]
    lifted = jnp.dot(
        second_all, in_full.reshape(model_width, 2 * unit_count), preferred_element_type=jnp.float32
    )
    lifted = lifted.reshape(length, 2, unit_count)
    inputs = lifted[:, 0]
    gate_vals = lifted[:, 1]
    activated = gelu_exact(inputs)
    hidden = (activated * gate_vals).astype(jnp.bfloat16)
    output = mixed_rows + lax.psum_scatter(
        jnp.dot(hidden, down_full, preferred_element_type=jnp.float32).astype(jnp.bfloat16),
        "mp",
        scatter_dimension=0,
        tiled=True,
    ).astype(jnp.float32)
    gain_two, in_full, down_full = feedforward_weights(mlp_gain, w_in, w_mlp_out)
    gain_one, qkv_full, out_full = attention_weights(attn_gain, w_qkv, w_attn_out)
    cot_all = lax.all_gather(cotangent, "mp", axis=0, tiled=True)
    hidden_grad = times_transposed(cot_all, down_full)
    down_grad = contract_rows(hidden, cot_all)
    input_grad = hidden_grad * gate_vals * gelu_slope(inputs)
    gate_grad = hidden_grad * activated
    lifted_grad = (
        jnp.stack([input_grad, gate_grad], axis=1)
        .astype(jnp.bfloat16)
        .reshape(length, 2 * unit_count)
    )
    in_grad = contract_rows(second_all, lifted_grad).reshape(model_width, 2, unit_count)
    in_flat = in_full.reshape(model_width, 2 * unit_count)
    second_grad = lax.psum_scatter(
        times_transposed(lifted_grad, in_flat), "mp", scatter_dimension=0, tiled=True
    )
    back_two, gain_two_part = norm_backward(
        second_grad, normed_two, inverse_two, gain_two.astype(jnp.float32)
    )
    mixed_grad = cotangent.astype(jnp.float32) + back_two
    mixed_low = mixed_grad.astype(jnp.bfloat16)
    mixed_all = lax.all_gather(mixed_low, "mp", axis=0, tiled=True)
    attended_grad = (
        times_transposed(mixed_all, out_full)
        .astype(jnp.bfloat16)
        .reshape(length, head_count, HEAD_DIM)
    )
    out_grad = contract_rows(attended_flat, mixed_all)
    query_grad, key_grad, value_grad = attention_backward(
        queries, key_rows, value_rows, attended, log_totals, attended_grad
    )
    query_grad = undo_rotary(query_grad, cosine_table, sine_table)
    key_grad = undo_rotary(key_grad, cosine_table, sine_table)
    projected_grad = (
        jnp.stack([query_grad, key_grad, value_grad], axis=1)
        .astype(jnp.bfloat16)
        .reshape(length, 3 * local_width)
    )
    qkv_grad = contract_rows(first_all, projected_grad).reshape(model_width, 3, local_width)
    qkv_flat = qkv_full.reshape(model_width, 3 * local_width)
    first_grad = lax.psum_scatter(
        times_transposed(projected_grad, qkv_flat).astype(jnp.bfloat16),
        "mp",
        scatter_dimension=0,
        tiled=True,
    ).astype(jnp.float32)
    back_one, gain_one_part = norm_backward(
        first_grad, normed_one, inverse_one, gain_one.astype(jnp.float32)
    )
    tokens_grad = mixed_grad + back_one
    down_shard, in_shard, gain_two_shard, out_shard, qkv_shard, gain_one_shard = (
        lax.psum_scatter(down_grad, "dp", scatter_dimension=1, tiled=True),
        lax.psum_scatter(in_grad, "dp", scatter_dimension=0, tiled=True),
        lax.psum_scatter(gain_two_part, "dp", scatter_dimension=0, tiled=True),
        lax.psum_scatter(out_grad, "dp", scatter_dimension=1, tiled=True),
        lax.psum_scatter(qkv_grad, "dp", scatter_dimension=0, tiled=True),
        lax.psum_scatter(gain_one_part, "dp", scatter_dimension=0, tiled=True),
    )
    gain_one_grad, gain_two_grad = lax.psum((gain_one_shard, gain_two_shard), "mp")
    return (
        output,
        tokens_grad,
        gain_one_grad,
        qkv_shard,
        out_shard,
        gain_two_grad,
        in_shard,
        down_shard,
    )


def nn(left, right):
    return lax.dot_general(left, right, (((1,), (0,)), ((), ())), preferred_element_type=F32)


def nt(left, right):
    return lax.dot_general(left, right, (((1,), (1,)), ((), ())), preferred_element_type=F32)


def tn(left, right):
    return lax.dot_general(left, right, (((0,), (0,)), ((), ())), preferred_element_type=F32)


def erf(x):
    return lax.erf(x)


def swap_halves(tile):
    lane = lax.broadcasted_iota(jnp.int32, tile.shape, 1)
    half = HEAD_DIM // 2
    back = pltpu.roll(tile, tile.shape[1] - half, 1)
    ahead = pltpu.roll(tile, half, 1)
    return jnp.where(lax.rem(lane, HEAD_DIM) < half, back, ahead)


def layer_kernel(
    ndp, heads,
    tok_h, cot_h, gain_a, gain_b, wq_h, wo_h, wi_h, wd_h, cos_h, sin_h,
    out_o, tg_o, ga_o, gb_o, dq_o, do_o, di_o, dd_o,
    wq_in, wo_in, wi_in, wd_in, cos_t, sin_t,
    gpad, gains, w1, w2, wf1, wf2, wof,
    xr, x1, x2, xc, x3, xt1, xt2, xtc, xt3,
    qk, vb, att, pbuf, hid, wide, hgrad_buf, lg, pg, gatt, dqs, dks, dvs,
    xh1, xh2, mixed, mgrad,
    rs_sc, rs_rc, rs_sy, rs_ry, rs_own,
    gs1, gr1, gz1, gy1, gw1,
    gs2, gr2, gz2, gy2, gw2,
    gv, gvr, ggs, ggr,
    send_sem, recv_sem, load_sem,
):
    nmp, rows, width = xr.shape
    length = nmp * rows
    na = ndp // PAIR
    dp = lax.axis_index("dp")
    mp = lax.axis_index("mp")
    za = dp // PAIR
    zb = lax.rem(dp, PAIR)
    core = lax.rem(mp, 2)
    ypos = mp // 2
    mate = mp + 1 - 2 * core
    ypeer = mp + 2 - 4 * ypos
    diag = mate + 2 - 4 * ypos
    xpeer = za * PAIR + (1 - zb)
    lw = heads * HEAD_DIM
    units = hid.shape[1]
    shard = w1.shape[0]
    cols_one, cols_two = w1.shape[1], w2.shape[1]

    def at_dp(d):
        return {"dp": d, "mp": mp}

    def at_mp(m):
        return {"dp": dp, "mp": m}

    counter = [0]
    sends = []

    def slot():
        counter[0] += 1
        return counter[0] - 1

    def put(src, dst, sem, dev):
        copy = pltpu.make_async_remote_copy(
            src_ref=src, dst_ref=dst, send_sem=send_sem.at[sem], recv_sem=recv_sem.at[sem],
            device_id=dev, device_id_type=MESH,
        )
        copy.start()
        sends.append(copy)

    def got(buf, sem):
        pltpu.make_async_remote_copy(
            src_ref=buf, dst_ref=buf, send_sem=send_sem.at[sem], recv_sem=recv_sem.at[sem],
            device_id=at_mp(mate), device_id_type=MESH,
        ).wait_recv()

    barrier = pltpu.get_barrier_semaphore()
    for k in range(1, ndp):
        pl.semaphore_signal(barrier, inc=1, device_id=at_dp(lax.rem(dp + k, ndp)), device_id_type=MESH)
    for other in (mate, ypeer, diag):
        pl.semaphore_signal(barrier, inc=1, device_id=at_mp(other), device_id_type=MESH)

    loads = [
        pltpu.make_async_copy(src, dst, load_sem.at[i])
        for i, (src, dst) in enumerate((
            (wq_h, wq_in), (tok_h, xr.at[mp]), (wo_h, wo_in), (wi_h, wi_in), (wd_h, wd_in),
            (cot_h, xc.at[mp]), (cos_h, cos_t), (sin_h, sin_t),
        ))
    ]
    for load in loads:
        load.start()

    def norm(vals):
        centered = vals - jnp.mean(vals, axis=-1, keepdims=True)
        inv = lax.rsqrt(jnp.mean(centered * centered, axis=-1, keepdims=True) + norm_eps)
        return centered * inv, inv

    def norm_back(grad, normed, inv, gain):
        scaled = grad * gain
        return inv * (
            scaled
            - jnp.mean(scaled, axis=-1, keepdims=True)
            - normed * jnp.mean(scaled * normed, axis=-1, keepdims=True)
        )

    def flip(vals):
        high, wide = vals.shape
        more_rows, more_cols = -high % 128, -wide % 128
        if more_cols:
            vals = jnp.concatenate([vals, jnp.zeros((high, more_cols), F32)], axis=1)
        if more_rows:
            vals = jnp.concatenate([vals, jnp.zeros((more_rows, wide + more_cols), F32)], axis=0)
        return vals.T[:wide, :high]

    def packed(q, k, v, o):
        parts = []
        for h in range(heads):
            parts += [q[:, h * HEAD_DIM : (h + 1) * HEAD_DIM], k[:, h * HEAD_DIM : (h + 1) * HEAD_DIM]]
        return jnp.concatenate([*parts, v, o], axis=1)

    gpad[...] = jnp.concatenate(
        [
            jnp.concatenate([gain_a[...].astype(F32), gain_b[...].astype(F32), jnp.zeros((6, shard), F32)], axis=0),
            jnp.zeros((8, 128 - shard), F32),
        ],
        axis=1,
    )
    loads[0].wait()
    loads[2].wait()
    w1[...] = packed(
        wq_in[0].astype(F32), wq_in[1].astype(F32), wq_in[2].astype(F32), flip(wo_in[...].astype(F32))
    ).astype(BF)
    loads[3].wait()
    loads[4].wait()
    w2[...] = jnp.concatenate(
        [
            wi_in[:, 0, :].astype(F32), wi_in[:, 1, :].astype(F32), flip(wd_in[...].astype(F32)),
            jnp.zeros((shard, cols_two - 3 * units), F32),
        ],
        axis=1,
    ).astype(BF)
    loads[1].wait()
    loads[5].wait()
    loads[6].wait()
    loads[7].wait()
    pl.semaphore_wait(barrier, ndp - 1 + 3)

    def gather_open(src, full, lo, hi):
        at = pl.ds(lo, hi - lo)
        return (src, full, at, [slot() for _ in range(na)], [slot() for _ in range(na)])

    def gather_far(state):
        src, full, at, zs, xs = state
        for k in (2, 1, 3):
            put(src.at[:, at], full.at[dp, :, at], zs[k], at_dp(lax.rem(za + k, na) * PAIR + zb))

    def gather_near(state):
        src, full, at, zs, xs = state
        put(src.at[:, at], full.at[dp, :, at], xs[0], at_dp(xpeer))

    def gather_forward(state, k):
        src, full, at, zs, xs = state
        source = lax.rem(za + na - k, na) * PAIR + zb
        got(full.at[source, :, at], zs[k])
        put(full.at[source, :, at], full.at[source, :, at], xs[k], at_dp(xpeer))

    def gather_end(state):
        src, full, at, zs, xs = state
        for k in range(na):
            source = lax.rem(za + na - k, na) * PAIR + (1 - zb)
            got(full.at[source, :, at], xs[k])

    order = (1, 3, 2)
    part_rows = rows // PARTS

    def part_at(p):
        return pl.ds(p * part_rows, part_rows)

    def spread_open(buf):
        return (buf, [[slot() for _ in range(3)] for _ in range(PARTS)])

    def spread_start(state, p):
        buf, sems = state
        block = buf.at[mp, part_at(p)]
        put(block, block, sems[p][0], at_mp(ypeer))
        put(block, block, sems[p][1], at_mp(mate))

    def spread_near(state):
        buf, sems = state
        for p in range(PARTS):
            got(buf.at[mate, part_at(p)], sems[p][1])

    def spread_forward(state, p):
        buf, sems = state
        block = buf.at[ypeer, part_at(p)]
        got(block, sems[p][0])
        put(block, block, sems[p][2], at_mp(mate))

    def spread_far(state):
        buf, sems = state
        for p in range(PARTS):
            got(buf.at[diag, part_at(p)], sems[p][2])

    def chunk(r):
        return pl.ds(pl.multiple_of(r * rows, rows), rows)

    def pair_rows(y):
        return pl.ds(pl.multiple_of(y * 2 * rows, 2 * rows), 2 * rows)

    near, far = pair_rows(ypos), pair_rows(1 - ypos)

    def pair_of(buf, y):
        return buf[pl.ds(pl.multiple_of(y * 2, 2), 2)].reshape(2 * rows, width)

    def scatter_open(i):
        return (i, [slot() for _ in range(PARTS)], slot(), [slot() for _ in range(PARTS)])

    def gain_part(part, x, r, row):
        if x is not None:
            gv[row : row + 1, :] += jnp.sum(part * x[r].astype(F32), axis=0, keepdims=True)

    def scatter_far(state, left, weights, x=None, row=0):
        i, s_far, s_near, s_y = state
        part = nt(left[chunk(diag), :], weights)
        rs_sc[i, 0] = part.astype(BF)
        for p in range(PARTS):
            at = part_at(p)
            put(rs_sc.at[i, 0, at], rs_rc.at[i, 0, at], s_far[p], at_mp(mate))
        gain_part(part, x, diag, row)
        part = nt(left[chunk(ypeer), :], weights)
        rs_own[i, 0] = part
        gain_part(part, x, ypeer, row)

    def scatter_send(state):
        i, s_far, s_near, s_y = state
        for p in range(PARTS):
            at = part_at(p)
            got(rs_rc.at[i, 0, at], s_far[p])
            rs_sy[i, at, :] = (rs_own[i, 0, at, :] + rs_rc[i, 0, at, :].astype(F32)).astype(BF)
            put(rs_sy.at[i, at], rs_ry.at[i, at], s_y[p], at_mp(ypeer))

    def scatter_near(state, left, weights, x=None, row=0):
        i, s_far, s_near, s_y = state
        part = nt(left[chunk(mate), :], weights)
        rs_sc[i, 1] = part.astype(BF)
        put(rs_sc.at[i, 1], rs_rc.at[i, 1], s_near, at_mp(mate))
        gain_part(part, x, mate, row)
        part = nt(left[chunk(mp), :], weights)
        rs_own[i, 1] = part
        gain_part(part, x, mp, row)

    def scatter_end(state, p):
        i, s_far, s_near, s_y = state
        at = part_at(p)
        if p == 0:
            got(rs_rc.at[i, 1], s_near)
        total = rs_own[i, 1, at, :] + rs_rc[i, 1, at, :].astype(F32)
        got(rs_ry.at[i, at], s_y[p])
        return total + rs_ry[i, at, :].astype(F32)

    def turn(buf, dst):
        @pl.loop(0, nmp)
        def _(r):
            cols = pl.ds(pl.multiple_of(r * rows, rows), rows)
            flipped = buf[r].T
            dst[:, :, :, cols] = flipped.reshape(na, PAIR, shard, rows)

    def product(xt, half, right):
        return nn(xt[:, half].reshape(na * shard, length), right).reshape(na, shard, right.shape[1])

    def grad_open(bufs, lo, hi):
        return (bufs, pl.ds(lo, hi - lo), [slot() for _ in range(na)], [slot() for _ in range(na)])

    def grad_start(state):
        (gs, gr, gz, gy, gw), at, xs, zs = state
        for k in (2, 1, 3, 0):
            a = lax.rem(za + k, na)
            put(gs.at[a, :, at], gr.at[a, :, at], xs[k], at_dp(xpeer))

    def grad_middle(state, k):
        (gs, gr, gz, gy, gw), at, xs, zs = state
        a = lax.rem(za + k, na)
        got(gr.at[a, :, at], xs[k])
        gz[k, :, at] = (gw[a, :, at] + gr[a, :, at].astype(F32)).astype(BF)
        put(gz.at[k, :, at], gy.at[k, :, at], zs[k], at_dp(a * PAIR + zb))

    def grad_end(state):
        (gs, gr, gz, gy, gw), at, xs, zs = state
        got(gr.at[za, :, at], xs[0])
        total = gw[za, :, at] + gr[za, :, at].astype(F32)
        for k in range(1, na):
            got(gy.at[k, :, at], zs[k])
            total = total + gy[k, :, at].astype(F32)
        return total

    one = (gs1, gr1, gz1, gy1, gw1)
    two = (gs2, gr2, gz2, gy2, gw2)

    gain_slots = [slot() for _ in range(ndp - 1)]
    for k in range(1, ndp):
        put(gpad, gains.at[dp], gain_slots[k - 1], at_dp(lax.rem(dp + k, ndp)))
    pieces = [gather_open(w1, wf1, c, c + 128) for c in range(0, cols_one, 128)]
    count_one = len(pieces)
    count_q = -(-3 * lw // 128)
    pieces += [gather_open(w2, wf2, c, c + 128) for c in range(0, cols_two, 128)]
    at_piece = [0]

    def pump(count):
        for _ in range(count):
            i = at_piece[0]
            if i >= len(pieces):
                return
            at_piece[0] += 1
            if i + AHEAD < len(pieces) and i < count_q:
                gather_far(pieces[i + AHEAD])
            if i + 1 < len(pieces) and i < count_q:
                gather_near(pieces[i + 1])
            for k in order:
                gather_forward(pieces[i], k)

    sp1 = spread_open(xr)
    gather_near(pieces[0])
    for i in range(AHEAD):
        gather_far(pieces[i])
        if i == 0:
            for p in range(PARTS):
                spread_start(sp1, p)
    gains[dp] = gpad[...]
    wf1[dp] = w1[...]
    wf2[dp] = w2[...]
    for k in range(1, ndp):
        source = lax.rem(dp + ndp - k, ndp)
        got(gains.at[source], gain_slots[k - 1])

    def whole_gain(i):
        return jnp.concatenate([gains[d, i : i + 1, :shard] for d in range(ndp)], axis=1)

    gain_one = whole_gain(0)
    gain_two = whole_gain(1)

    normed_one, inv_one = norm(xr[mp].astype(F32))
    xh1[...] = normed_one
    x1[mp] = (normed_one * gain_one).astype(BF)

    def first_norm(r):
        x1[r] = (norm(xr[r].astype(F32))[0] * gain_one).astype(BF)

    pump(1)
    spread_near(sp1)
    first_norm(mate)
    spc = spread_open(xc)
    pump(1)
    for p in range(PARTS):
        spread_forward(sp1, p)
        spread_start(spc, p)
    first_norm(ypeer)
    pump(1)
    spread_far(sp1)
    first_norm(diag)
    turn(x1, xt1)
    pump(count_q - 2)
    for p in range(PARTS):
        spread_forward(spc, p)
    for piece in pieces[count_q + AHEAD :]:
        gather_far(piece)
    for piece in pieces[count_q + 1 :]:
        gather_near(piece)
    for i in range(count_q):
        gather_end(pieces[i])

    wide[:, : 3 * lw] = nn(
        x1[...].reshape(length, width), wf1[:, :, : 3 * lw].reshape(width, 3 * lw)
    )

    @pl.loop(0, nmp)
    def _(r):
        at = chunk(r)
        for h in range(heads):
            t = slice(h * 128, (h + 1) * 128)
            u = wide[at, t]
            qk[at, t] = (u * cos_t[at, :] + swap_halves(u) * sin_t[at, :]).astype(BF)
        vb[at, :] = wide[at, 2 * lw : 3 * lw].astype(BF)

    scale = HEAD_DIM ** (-0.5)

    def query(h, at=slice(None)):
        return qk[at, h * 128 : h * 128 + HEAD_DIM]

    def key(h, at=slice(None)):
        return qk[at, h * 128 + HEAD_DIM : (h + 1) * 128]

    def value(h, at=slice(None)):
        return vb[at, h * HEAD_DIM : (h + 1) * HEAD_DIM]

    def attend(at):
        outs = []
        for h in range(heads):
            scores = nt(query(h, at), key(h)) * scale
            peak = jnp.max(scores, axis=-1, keepdims=True)
            e = jnp.exp(scores - peak)
            probs = e / jnp.sum(e, axis=-1, keepdims=True)
            pbuf[h, at, :] = probs
            outs.append(nn(probs.astype(BF), value(h)))
        att[at, :] = jnp.concatenate(outs, axis=1).astype(BF)

    pump(1)
    attend(far)
    pump(1)
    for i in range(count_q, count_one):
        gather_end(pieces[i])
    wof[...] = wf1[:, :, 3 * lw :].reshape(width, lw)
    rs_a = scatter_open(0)
    scatter_far(rs_a, att, wof[...])
    scatter_send(rs_a)
    attend(near)
    scatter_near(rs_a, att, wof[...])
    pump(1)
    spread_near(spc)
    spread_far(spc)
    turn(xc, xtc)
    pump(2)

    inv_two = []
    sp2 = spread_open(x2)
    for p in range(PARTS):
        at = part_at(p)
        mixed[at, :] = xr[mp, at, :].astype(F32) + scatter_end(rs_a, p)
        normed_two, inv = norm(mixed[at, :])
        inv_two.append(inv)
        xh2[at, :] = normed_two
        x2[mp, at, :] = (normed_two * gain_two).astype(BF)
        spread_start(sp2, p)
    def gelu_part(y, at):
        wide[at, : 2 * units] = nn(
            pair_of(x2, y), wf2[:, :, : 2 * units].reshape(width, 2 * units)
        )
        hgrad_buf[at, :] = nn(
            pair_of(xc, y), wf2[:, :, 2 * units : 3 * units].reshape(width, units)
        )

        @pl.loop(0, 2)
        def _(r):
            now = chunk(2 * y + r)
            u = wide[now, :units]
            gate = wide[now, units : 2 * units]
            cdf = 0.5 * (1.0 + erf(u * 0.7071067811865476))
            act = u * cdf
            slope = cdf + u * jnp.exp(-0.5 * u * u) * 0.3989422804014327
            hid[now, :] = (act * gate).astype(BF)
            hgrad = hgrad_buf[now, :]
            lg[now, :] = jnp.concatenate([hgrad * gate * slope, hgrad * act], axis=1).astype(BF)

    pump(1)
    spread_near(sp2)
    pump(1)
    for p in range(PARTS):
        spread_forward(sp2, p)
    spread_far(sp2)
    turn(x2, xt2)
    pump(len(pieces))
    for piece in pieces[count_one:]:
        gather_end(piece)
    gelu_part(ypos, near)
    gelu_part(1 - ypos, far)
    in_flat = wf2[:, :, : 2 * units].reshape(width, 2 * units)
    rs_g = scatter_open(1)
    gv[...] = jnp.zeros_like(gv)
    scatter_far(rs_g, lg, in_flat, x2, 1)
    g_two = [grad_open(two, c, c + 128) for c in range(0, cols_two, 128)]
    early = 2 * units // 128
    steps = []

    waiting = []
    flying = [0]

    def leave(state):
        steps.extend((state, k) for k in (2, 1, 3))
        if flying[0] < WINDOW:
            flying[0] += 1
            grad_start(state)
        else:
            waiting.append(state)

    def reduce_steps(count):
        for _ in range(min(count, len(steps))):
            state, k = steps.pop(0)
            grad_middle(state, k)
            if k == 3:
                if waiting:
                    grad_start(waiting.pop(0))
                else:
                    flying[0] -= 1

    gs2[:, :, : 2 * units] = product(xt2, 1 - zb, lg[...]).astype(BF)
    for g in g_two[:early]:
        leave(g)
    scatter_send(rs_g)
    gs2[:, :, 2 * units : 3 * units] = product(xtc, 1 - zb, hid[...]).astype(BF)
    gs2[:, :, 3 * units :] = jnp.zeros((na, shard, cols_two - 3 * units), BF)
    for g in g_two[early:]:
        leave(g)
    scatter_near(rs_g, lg, in_flat, x2, 1)
    gw2[:, :, : 2 * units] = product(xt2, zb, lg[...])
    gw2[:, :, 2 * units : 3 * units] = product(xtc, zb, hid[...])
    gw2[:, :, 3 * units :] = jnp.zeros((na, shard, cols_two - 3 * units), F32)
    down_flat = wf2[:, :, 2 * units : 3 * units].reshape(width, units)
    rs_o = scatter_open(3)
    scatter_far(rs_o, hid, down_flat)
    scatter_near(rs_o, hid, down_flat)
    reduce_steps(6)
    sp3 = spread_open(x3)
    for p in range(PARTS):
        at = part_at(p)
        back_two = norm_back(scatter_end(rs_g, p), xh2[at, :], inv_two[p], gain_two)
        mgrad[at, :] = xc[mp, at, :].astype(F32) + back_two
        x3[mp, at, :] = mgrad[at, :].astype(BF)
        spread_start(sp3, p)
    scatter_send(rs_o)
    reduce_steps(4)
    spread_near(sp3)

    def attend_back(y, at, h, first):
        g = gatt[at, h * HEAD_DIM : (h + 1) * HEAD_DIM]
        o = att[at, h * HEAD_DIM : (h + 1) * HEAD_DIM]
        probs = pbuf[h, at, :]
        dv = tn(probs.astype(BF), g)
        dprobs = nt(g, value(h))
        delta = jnp.sum(g.astype(F32) * o.astype(F32), axis=-1, keepdims=True)
        ds = (probs * (dprobs - delta) * scale).astype(BF)
        dqs[h, at, :] = nn(ds, key(h))
        dk = tn(ds, query(h, at))
        if first:
            dvs[h] = dv
            dks[h] = dk
        else:
            dvs[h] += dv
            dks[h] += dk

    gatt[near, :] = nn(pair_of(x3, ypos), wof[...]).astype(BF)
    for h in range(heads):
        attend_back(ypos, near, h, True)
        reduce_steps(1)
    for p in range(PARTS):
        spread_forward(sp3, p)
    reduce_steps(5)
    spread_far(sp3)
    gatt[far, :] = nn(pair_of(x3, 1 - ypos), wof[...]).astype(BF)
    turn(x3, xt3)
    late = -(-3 * lw // 128) * 128
    gs1[:, :, 3 * lw :] = product(xt3, 1 - zb, att[...]).astype(BF)
    g_one = {c: grad_open(one, c, c + 128) for c in range(0, cols_one, 128)}
    for c in range(late, cols_one, 128):
        leave(g_one[c])
    gw1[:, :, 3 * lw :] = product(xt3, zb, att[...])
    done = 2 * lw
    for h in range(heads):
        attend_back(1 - ypos, far, h, False)
        t = slice(h * 128, (h + 1) * 128)
        v = slice(2 * lw + h * HEAD_DIM, 2 * lw + (h + 1) * HEAD_DIM)

        @pl.loop(0, nmp)
        def _(r):
            at = chunk(r)
            u = jnp.concatenate([dqs[h, at, :], dks[h, at, :]], axis=1)
            pg[at, t] = (u * cos_t[at, :] - swap_halves(u) * sin_t[at, :]).astype(BF)
            pg[at, v] = dvs[h, at, :].astype(BF)

        gs1[:, :, t] = product(xt1, 1 - zb, pg[:, t]).astype(BF)
        leave(g_one[h * 128])
        last = h == heads - 1
        end = late if last else (2 * lw + (h + 1) * HEAD_DIM) // 128 * 128
        if end > done:
            ready = slice(done, min(end, 3 * lw))
            gs1[:, :, ready] = product(xt1, 1 - zb, pg[:, ready]).astype(BF)
            for c in range(done, end, 128):
                leave(g_one[c])
            gw1[:, :, ready] = product(xt1, zb, pg[:, ready])
            done = end
        gw1[:, :, t] = product(xt1, zb, pg[:, t])
        reduce_steps(3)

    qkv_flat = wf1[:, :, : 3 * lw].reshape(width, 3 * lw)
    rs_f = scatter_open(2)
    scatter_far(rs_f, pg, qkv_flat, x1, 0)
    reduce_steps(3)
    scatter_send(rs_f)
    scatter_near(rs_f, pg, qkv_flat, x1, 0)
    gain_sems = [slot() for _ in range(3)]
    for k, other in enumerate((ypeer, mate, diag)):
        put(gv, gvr.at[k], gain_sems[k], at_mp(other))
    reduce_steps(99)
    gain_sum = gv[...]
    for k in range(3):
        got(gvr.at[k], gain_sems[k])
        gain_sum = gain_sum + gvr[k]
    empty = jnp.zeros((8, 128 - shard), F32)
    for d in range(ndp):
        ggs[d] = jnp.concatenate([gain_sum[:, d * shard : (d + 1) * shard], empty], axis=1)
    sum_sems = [slot() for _ in range(ndp)]
    for k in range(1, ndp):
        d = lax.rem(dp + k, ndp)
        put(ggs.at[d], ggr.at[k], sum_sems[k], at_dp(d))

    for p in range(PARTS):
        at = part_at(p)
        out_o[at, :] = mixed[at, :] + scatter_end(rs_o, p)
    total_two = jnp.concatenate([grad_end(g) for g in g_two], axis=1)
    for i in range(2):
        di_o[:, i, :] = total_two[:, i * units : (i + 1) * units]
    dd_o[...] = flip(total_two[:, 2 * units : 3 * units])
    for p in range(PARTS):
        at = part_at(p)
        own_inv = inv_one[p * part_rows : (p + 1) * part_rows]
        back_one = norm_back(scatter_end(rs_f, p), xh1[at, :], own_inv, gain_one)
        tg_o[at, :] = mgrad[at, :] + back_one
    one_total = {c: grad_end(g) for c, g in sorted(g_one.items())}
    qk_total = [one_total[h * 128] for h in range(heads)]
    vo_total = jnp.concatenate([one_total[c] for c in range(2 * lw, cols_one, 128)], axis=1)
    dq_o[0] = jnp.concatenate([t[:, :HEAD_DIM] for t in qk_total], axis=1)
    dq_o[1] = jnp.concatenate([t[:, HEAD_DIM:] for t in qk_total], axis=1)
    dq_o[2] = vo_total[:, :lw]
    do_o[...] = flip(vo_total[:, lw:])
    total = ggs[dp]
    for k in range(1, ndp):
        got(ggr.at[k], sum_sems[k])
        total = total + ggr[k]
    ga_o[...] = total[0:1, :shard] / gain_a[...].astype(F32)
    gb_o[...] = total[1:2, :shard] / gain_b[...].astype(F32)
    for copy in sends:
        copy.wait_send()


def settle_kernel(*refs):
    count = (len(refs) - 1) // 2
    sems = refs[-1]
    copies = [
        pltpu.make_async_copy(src, dst, sems.at[i])
        for i, (src, dst) in enumerate(zip(refs[:count], refs[count:-1]))
    ]
    for copy in copies:
        copy.start()
    for copy in copies:
        copy.wait()


def fused_shards(tokens, cotangent, attn_gain, w_qkv, w_attn_out, mlp_gain, w_in, w_mlp_out):
    ndp = lax.axis_size("dp")
    nmp = lax.axis_size("mp")
    rows, width = tokens.shape
    shard = w_qkv.shape[0]
    lw = w_qkv.shape[2]
    units = w_in.shape[2]
    heads = lw // HEAD_DIM
    length = rows * nmp
    na = ndp // PAIR
    half = HEAD_DIM // 2
    cols_one = 4 * lw
    cols_two = -(-3 * units // 128) * 128
    freqs = rope_base ** (-(np.arange(half, dtype=np.float32) * np.float32(2.0) / HEAD_DIM))
    angles = np.arange(length, dtype=np.float32)[:, None] * freqs.astype(np.float32)[None, :]
    cos_t = np.tile(np.cos(angles).astype(np.float32), (1, 128 // half))
    sin = np.sin(angles).astype(np.float32)
    sin_t = np.tile(np.concatenate([-sin, sin], axis=1), (1, 128 // HEAD_DIM))

    def buf(shape, dtype=BF):
        return pltpu.VMEM(shape, dtype)

    def grad_bufs(cols):
        return [
            buf((na, shard, cols)), buf((na, shard, cols)), buf((na, shard, cols)),
            buf((na, shard, cols)), buf((na, shard, cols), F32),
        ]

    nsem = 2 * ndp + 2 * na * (cols_one + cols_two) // 128 + 4 * (3 * PARTS) + 4 * (2 * PARTS + 1) + 2 * na * (cols_one + cols_two) // 128 + 8
    scratch = [
        buf((3, shard, lw)), buf((lw, shard)), buf((shard, 2, units)), buf((units, shard)),
        buf((length, 128), F32), buf((length, 128), F32),
        buf((8, 128), F32), buf((ndp, 8, 128), F32),
        buf((shard, cols_one)), buf((shard, cols_two)),
        buf((ndp, shard, cols_one)), buf((ndp, shard, cols_two)), buf((width, lw)),
        *[buf((nmp, rows, width)) for _ in range(5)],
        *[buf((na, PAIR, shard, length)) for _ in range(4)],
        buf((length, heads * 128)), buf((length, lw)), buf((length, lw)),
        buf((heads, length, length), F32), buf((length, units)),
        buf((length, max(3 * lw, 2 * units)), F32), buf((length, units), F32),
        buf((length, 2 * units)), buf((length, 3 * lw)), buf((length, lw)),
        *[buf((heads, length, HEAD_DIM), F32) for _ in range(3)],
        *[buf((rows, width), F32) for _ in range(4)],
        buf((4, 2, rows, width)), buf((4, 2, rows, width)),
        buf((4, rows, width)), buf((4, rows, width)), buf((4, 2, rows, width), F32),
        *grad_bufs(cols_one), *grad_bufs(cols_two),
        buf((8, width), F32), buf((3, 8, width), F32), buf((ndp, 8, 128), F32), buf((ndp, 8, 128), F32),
        pltpu.SemaphoreType.DMA((nsem,)), pltpu.SemaphoreType.DMA((nsem,)),
        pltpu.SemaphoreType.DMA((8,)),
    ]
    vmem = pl.BlockSpec(memory_space=pltpu.VMEM)
    hbm = pl.BlockSpec(memory_space=pl.ANY)
    shapes = [
        (rows, width), (rows, width), (1, shard), (1, shard), (3, shard, lw), (lw, shard),
        (shard, 2, units), (units, shard),
    ]
    results = pl.pallas_call(
        functools.partial(layer_kernel, ndp, heads),
        out_shape=[buf(s, F32) for s in shapes],
        in_specs=[hbm, hbm, vmem, vmem, hbm, hbm, hbm, hbm, hbm, hbm],
        out_specs=[vmem] * 8,
        scratch_shapes=scratch,
        compiler_params=pltpu.CompilerParams(
            collective_id=0, has_side_effects=True, vmem_limit_bytes=56 * 1024 * 1024
        ),
    )(
        tokens, cotangent, attn_gain.reshape(1, shard), mlp_gain.reshape(1, shard),
        w_qkv.transpose(1, 0, 2), w_attn_out, w_in, w_mlp_out,
        jnp.asarray(cos_t), jnp.asarray(sin_t),
    )
    out, tg, ga, gb, dq, do, di, dd = pl.pallas_call(
        settle_kernel,
        out_shape=[jax.ShapeDtypeStruct(s, F32) for s in shapes],
        in_specs=[vmem] * 8,
        out_specs=[hbm] * 8,
        scratch_shapes=[pltpu.SemaphoreType.DMA((8,))],
    )(*[pltpu.with_memory_space_constraint(r, pltpu.VMEM) for r in results])
    return (
        out, tg, ga.reshape(shard), dq.transpose(1, 0, 2), do, gb.reshape(shard), di, dd,
    )


def choose(tokens, cotangent, attn_gain, w_qkv, w_attn_out, mlp_gain, w_in, w_mlp_out):
    ndp = lax.axis_size("dp")
    shard = w_qkv.shape[0]
    fits = (
        lax.axis_size("mp") == 4
        and ndp % PAIR == 0
        and shard % 16 == 0
        and shard <= 128
        and w_mlp_out.shape[1] == shard
        and tokens.shape[0] % 128 == 0
        and tokens.shape[0] <= 128
        and 4 * w_qkv.shape[2] % 128 == 0
        and w_qkv.shape[2] % HEAD_DIM == 0
    )
    form = fused_shards if fits else shards
    return form(tokens, cotangent, attn_gain, w_qkv, w_attn_out, mlp_gain, w_in, w_mlp_out)


def solution(mesh):
    in_specs = (
        P(("dp", "mp"), None),
        P(("dp", "mp"), None),
        P("dp"),
        P("dp", None, "mp"),
        P("mp", "dp"),
        P("dp"),
        P("dp", None, "mp"),
        P("mp", "dp"),
    )
    out_specs = (
        P(("dp", "mp"), None),
        P(("dp", "mp"), None),
        P("dp"),
        P("dp", None, "mp"),
        P("mp", "dp"),
        P("dp"),
        P("dp", None, "mp"),
        P("mp", "dp"),
    )
    return jax.shard_map(choose, mesh=mesh, in_specs=in_specs, out_specs=out_specs, check_vma=False)
```

```python
import functools

import jax
import jax.numpy as jnp
import numpy as np
from jax import lax
from jax.experimental import pallas as pl
from jax.experimental.pallas import tpu as pltpu
from jax.sharding import PartitionSpec as P

MESH = pl.DeviceIdType.MESH
PAIR = 2
PARTS = 2
AHEAD = 2
WINDOW = 2
BF = jnp.bfloat16
F32 = jnp.float32

HEAD_DIM = 64


norm_eps = 1e-05
rope_base = 160000.0
query_block = 512


def rotary_tables(length, head_width):
    half_width = head_width // 2
    freqs = rope_base ** (-(jnp.arange(half_width, dtype=jnp.float32) * 2.0 / head_width))
    angles = jnp.arange(length, dtype=jnp.float32)[:, None] * freqs[None, :]
    angles = jnp.concatenate([angles, angles], axis=1)
    return (jnp.cos(angles), jnp.sin(angles))


def rotate_half(values):
    half_width = values.shape[-1] // 2
    return jnp.concatenate([-values[..., half_width:], values[..., :half_width]], axis=-1)


def apply_rotary(values, cosine_table, sine_table):
    return values * cosine_table[:, None, :] + rotate_half(values) * sine_table[:, None, :]


def undo_rotary(grads, cosine_table, sine_table):
    return grads * cosine_table[:, None, :] - rotate_half(grads * sine_table[:, None, :])


def norm_stats(values):
    centered = values - jnp.mean(values, axis=-1, keepdims=True)
    variance = jnp.mean(centered * centered, axis=-1, keepdims=True)
    inverse = lax.rsqrt(variance + norm_eps)
    return (centered * inverse, inverse)


def norm_backward(grad_out, normed, inverse, gain_vals):
    scaled = grad_out * gain_vals
    grad_in = inverse * (
        scaled
        - jnp.mean(scaled, axis=-1, keepdims=True)
        - normed * jnp.mean(scaled * normed, axis=-1, keepdims=True)
    )
    return (grad_in, jnp.sum(grad_out * normed, axis=0))


def gelu_exact(values):
    return 0.5 * values * (1.0 + jax.scipy.special.erf(values * 0.7071067811865476))


def gelu_slope(values):
    return (
        0.5 * (1.0 + jax.scipy.special.erf(values * 0.7071067811865476))
        + values * jnp.exp(-0.5 * values * values) * 0.3989422804014327
    )


def contract_rows(left, right):
    return lax.dot_general(
        left, right, (((0,), (0,)), ((), ())), preferred_element_type=jnp.float32
    )


def times_transposed(left, right):
    return lax.dot_general(
        left, right, (((1,), (1,)), ((), ())), preferred_element_type=jnp.float32
    )


def attention_weights(attn_gain, w_qkv, w_attn_out):
    return (
        lax.all_gather(attn_gain, "dp", axis=0, tiled=True),
        lax.all_gather(w_qkv, "dp", axis=0, tiled=True),
        lax.all_gather(w_attn_out, "dp", axis=1, tiled=True),
    )


def feedforward_weights(mlp_gain, w_in, w_mlp_out):
    return (
        lax.all_gather(mlp_gain, "dp", axis=0, tiled=True),
        lax.all_gather(w_in, "dp", axis=0, tiled=True),
        lax.all_gather(w_mlp_out, "dp", axis=1, tiled=True),
    )


def attention_forward(queries, key_rows, value_rows):
    length, head_count, head_width = queries.shape
    block_size = min(query_block, length)
    score_scale = head_width ** (-0.5)
    blocks = queries.reshape(length // block_size, block_size, head_count, head_width)

    def one_block(block_rows):
        scores = (
            jnp.einsum("qhd,khd->hqk", block_rows, key_rows, preferred_element_type=jnp.float32)
            * score_scale
        )
        row_peak = jnp.max(scores, axis=-1, keepdims=True)
        exp_scores = jnp.exp(scores - row_peak)
        row_total = jnp.sum(exp_scores, axis=-1, keepdims=True)
        attn_probs = (exp_scores / row_total).astype(jnp.bfloat16)
        block_out = jnp.einsum(
            "hqk,khd->qhd", attn_probs, value_rows, preferred_element_type=jnp.float32
        )
        return (block_out.astype(jnp.bfloat16), (row_peak + jnp.log(row_total))[..., 0])

    outs, log_totals = lax.map(one_block, blocks)
    return (outs.reshape(length, head_count, head_width), log_totals)


def attention_backward(queries, key_rows, value_rows, attended, log_totals, grad_out):
    length, head_count, head_width = queries.shape
    block_size = min(query_block, length)
    nblocks = length // block_size
    score_scale = head_width ** (-0.5)

    def one_block(running, block_inputs):
        key_grad, value_grad = running
        block_rows, out_rows, grad_rows, lse_rows = block_inputs
        scores = (
            jnp.einsum("qhd,khd->hqk", block_rows, key_rows, preferred_element_type=jnp.float32)
            * score_scale
        )
        attn_probs = jnp.exp(scores - lse_rows[..., None])
        value_grad = value_grad + jnp.einsum(
            "hqk,qhd->khd",
            attn_probs.astype(jnp.bfloat16),
            grad_rows,
            preferred_element_type=jnp.float32,
        )
        dprobs = jnp.einsum(
            "qhd,khd->hqk", grad_rows, value_rows, preferred_element_type=jnp.float32
        )
        row_delta = jnp.sum(grad_rows.astype(jnp.float32) * out_rows.astype(jnp.float32), axis=-1).T
        dscores = (attn_probs * (dprobs - row_delta[..., None]) * score_scale).astype(jnp.bfloat16)
        query_grad = jnp.einsum(
            "hqk,khd->qhd", dscores, key_rows, preferred_element_type=jnp.float32
        )
        key_grad = key_grad + jnp.einsum(
            "hqk,qhd->khd", dscores, block_rows, preferred_element_type=jnp.float32
        )
        return ((key_grad, value_grad), query_grad)

    zero_grad = jnp.zeros((length, head_count, head_width), jnp.float32)
    shape_blocks = (nblocks, block_size, head_count, head_width)
    block_inputs = (
        queries.reshape(shape_blocks),
        attended.reshape(shape_blocks),
        grad_out.reshape(shape_blocks),
        log_totals,
    )
    (key_grad, value_grad), query_grad = lax.scan(one_block, (zero_grad, zero_grad), block_inputs)
    return (query_grad.reshape(length, head_count, head_width), key_grad, value_grad)


def shards(tokens, cotangent, attn_gain, w_qkv, w_attn_out, mlp_gain, w_in, w_mlp_out):
    gain_one, qkv_full, out_full = attention_weights(attn_gain, w_qkv, w_attn_out)
    gain_two, in_full, down_full = feedforward_weights(mlp_gain, w_in, w_mlp_out)
    model_width = tokens.shape[1]
    residual = tokens.astype(jnp.float32)
    normed_one, inverse_one = norm_stats(residual)
    first_in = (normed_one * gain_one.astype(jnp.float32)).astype(jnp.bfloat16)
    first_all = lax.all_gather(first_in, "mp", axis=0, tiled=True)
    length = first_all.shape[0]
    local_width = qkv_full.shape[2]
    head_count = local_width // HEAD_DIM
    cosine_table, sine_table = rotary_tables(length, HEAD_DIM)
    projected = jnp.dot(
        first_all,
        qkv_full.reshape(model_width, 3 * local_width),
        preferred_element_type=jnp.float32,
    )
    projected = projected.reshape(length, 3, head_count, HEAD_DIM)
    queries = apply_rotary(projected[:, 0], cosine_table, sine_table).astype(jnp.bfloat16)
    key_rows = apply_rotary(projected[:, 1], cosine_table, sine_table).astype(jnp.bfloat16)
    value_rows = projected[:, 2].astype(jnp.bfloat16)
    attended, log_totals = attention_forward(queries, key_rows, value_rows)
    attended_flat = attended.reshape(length, local_width)
    mixed_rows = residual + lax.psum_scatter(
        jnp.dot(attended_flat, out_full, preferred_element_type=jnp.float32),
        "mp",
        scatter_dimension=0,
        tiled=True,
    )
    normed_two, inverse_two = norm_stats(mixed_rows)
    second_in = (normed_two * gain_two.astype(jnp.float32)).astype(jnp.bfloat16)
    second_all = lax.all_gather(second_in, "mp", axis=0, tiled=True)
    unit_count = in_full.shape[2]
    lifted = jnp.dot(
        second_all, in_full.reshape(model_width, 2 * unit_count), preferred_element_type=jnp.float32
    )
    lifted = lifted.reshape(length, 2, unit_count)
    inputs = lifted[:, 0]
    gate_vals = lifted[:, 1]
    activated = gelu_exact(inputs)
    hidden = (activated * gate_vals).astype(jnp.bfloat16)
    output = mixed_rows + lax.psum_scatter(
        jnp.dot(hidden, down_full, preferred_element_type=jnp.float32).astype(jnp.bfloat16),
        "mp",
        scatter_dimension=0,
        tiled=True,
    ).astype(jnp.float32)
    gain_two, in_full, down_full = feedforward_weights(mlp_gain, w_in, w_mlp_out)
    gain_one, qkv_full, out_full = attention_weights(attn_gain, w_qkv, w_attn_out)
    cot_all = lax.all_gather(cotangent, "mp", axis=0, tiled=True)
    hidden_grad = times_transposed(cot_all, down_full)
    down_grad = contract_rows(hidden, cot_all)
    input_grad = hidden_grad * gate_vals * gelu_slope(inputs)
    gate_grad = hidden_grad * activated
    lifted_grad = (
        jnp.stack([input_grad, gate_grad], axis=1)
        .astype(jnp.bfloat16)
        .reshape(length, 2 * unit_count)
    )
    in_grad = contract_rows(second_all, lifted_grad).reshape(model_width, 2, unit_count)
    in_flat = in_full.reshape(model_width, 2 * unit_count)
    second_grad = lax.psum_scatter(
        times_transposed(lifted_grad, in_flat), "mp", scatter_dimension=0, tiled=True
    )
    back_two, gain_two_part = norm_backward(
        second_grad, normed_two, inverse_two, gain_two.astype(jnp.float32)
    )
    mixed_grad = cotangent.astype(jnp.float32) + back_two
    mixed_low = mixed_grad.astype(jnp.bfloat16)
    mixed_all = lax.all_gather(mixed_low, "mp", axis=0, tiled=True)
    attended_grad = (
        times_transposed(mixed_all, out_full)
        .astype(jnp.bfloat16)
        .reshape(length, head_count, HEAD_DIM)
    )
    out_grad = contract_rows(attended_flat, mixed_all)
    query_grad, key_grad, value_grad = attention_backward(
        queries, key_rows, value_rows, attended, log_totals, attended_grad
    )
    query_grad = undo_rotary(query_grad, cosine_table, sine_table)
    key_grad = undo_rotary(key_grad, cosine_table, sine_table)
    projected_grad = (
        jnp.stack([query_grad, key_grad, value_grad], axis=1)
        .astype(jnp.bfloat16)
        .reshape(length, 3 * local_width)
    )
    qkv_grad = contract_rows(first_all, projected_grad).reshape(model_width, 3, local_width)
    qkv_flat = qkv_full.reshape(model_width, 3 * local_width)
    first_grad = lax.psum_scatter(
        times_transposed(projected_grad, qkv_flat).astype(jnp.bfloat16),
        "mp",
        scatter_dimension=0,
        tiled=True,
    ).astype(jnp.float32)
    back_one, gain_one_part = norm_backward(
        first_grad, normed_one, inverse_one, gain_one.astype(jnp.float32)
    )
    tokens_grad = mixed_grad + back_one
    down_shard, in_shard, gain_two_shard, out_shard, qkv_shard, gain_one_shard = (
        lax.psum_scatter(down_grad, "dp", scatter_dimension=1, tiled=True),
        lax.psum_scatter(in_grad, "dp", scatter_dimension=0, tiled=True),
        lax.psum_scatter(gain_two_part, "dp", scatter_dimension=0, tiled=True),
        lax.psum_scatter(out_grad, "dp", scatter_dimension=1, tiled=True),
        lax.psum_scatter(qkv_grad, "dp", scatter_dimension=0, tiled=True),
        lax.psum_scatter(gain_one_part, "dp", scatter_dimension=0, tiled=True),
    )
    gain_one_grad, gain_two_grad = lax.psum((gain_one_shard, gain_two_shard), "mp")
    return (
        output,
        tokens_grad,
        gain_one_grad,
        qkv_shard,
        out_shard,
        gain_two_grad,
        in_shard,
        down_shard,
    )


def nn(left, right):
    return lax.dot_general(left, right, (((1,), (0,)), ((), ())), preferred_element_type=F32)


def nt(left, right):
    return lax.dot_general(left, right, (((1,), (1,)), ((), ())), preferred_element_type=F32)


def tn(left, right):
    return lax.dot_general(left, right, (((0,), (0,)), ((), ())), preferred_element_type=F32)


def erf(x):
    return lax.erf(x)


def swap_halves(tile):
    lane = lax.broadcasted_iota(jnp.int32, tile.shape, 1)
    half = HEAD_DIM // 2
    back = pltpu.roll(tile, tile.shape[1] - half, 1)
    ahead = pltpu.roll(tile, half, 1)
    return jnp.where(lax.rem(lane, HEAD_DIM) < half, back, ahead)


def layer_kernel(
    ndp, heads,
    tok_h, cot_h, gain_a, gain_b, wq_h, wo_h, wi_h, wd_h, cos_h, sin_h,
    out_o, tg_o, ga_o, gb_o, dq_o, do_o, di_o, dd_o,
    wq_in, wo_in, wi_in, wd_in, cos_t, sin_t,
    gpad, gains, w1, w2, wf1, wf2, wof,
    xr, x1, x2, xc, x3, xt1, xt2, xtc, xt3,
    qk, vb, att, pbuf, hid, wide, hgrad_buf, lg, pg, gatt, dqs, dks, dvs,
    xh1, xh2, mixed, mgrad,
    rs_sc, rs_rc, rs_sy, rs_ry, rs_own,
    gs1, gr1, gz1, gy1, gw1,
    gs2, gr2, gz2, gy2, gw2,
    gv, gvr, ggs, ggr,
    send_sem, recv_sem, load_sem,
):
    nmp, rows, width = xr.shape
    length = nmp * rows
    na = ndp // PAIR
    dp = lax.axis_index("dp")
    mp = lax.axis_index("mp")
    za = dp // PAIR
    zb = lax.rem(dp, PAIR)
    core = lax.rem(mp, 2)
    ypos = mp // 2
    mate = mp + 1 - 2 * core
    ypeer = mp + 2 - 4 * ypos
    diag = mate + 2 - 4 * ypos
    xpeer = za * PAIR + (1 - zb)
    lw = heads * HEAD_DIM
    units = hid.shape[1]
    shard = w1.shape[0]
    cols_one, cols_two = w1.shape[1], w2.shape[1]

    def at_dp(d):
        return {"dp": d, "mp": mp}

    def at_mp(m):
        return {"dp": dp, "mp": m}

    counter = [0]
    sends = []

    def slot():
        counter[0] += 1
        return counter[0] - 1

    def put(src, dst, sem, dev):
        copy = pltpu.make_async_remote_copy(
            src_ref=src, dst_ref=dst, send_sem=send_sem.at[sem], recv_sem=recv_sem.at[sem],
            device_id=dev, device_id_type=MESH,
        )
        copy.start()
        sends.append(copy)

    def got(buf, sem):
        pltpu.make_async_remote_copy(
            src_ref=buf, dst_ref=buf, send_sem=send_sem.at[sem], recv_sem=recv_sem.at[sem],
            device_id=at_mp(mate), device_id_type=MESH,
        ).wait_recv()

    barrier = pltpu.get_barrier_semaphore()
    for k in range(1, ndp):
        pl.semaphore_signal(barrier, inc=1, device_id=at_dp(lax.rem(dp + k, ndp)), device_id_type=MESH)
    for other in (mate, ypeer, diag):
        pl.semaphore_signal(barrier, inc=1, device_id=at_mp(other), device_id_type=MESH)

    loads = [
        pltpu.make_async_copy(src, dst, load_sem.at[i])
        for i, (src, dst) in enumerate((
            (wq_h, wq_in), (tok_h, xr.at[mp]), (wo_h, wo_in), (wi_h, wi_in), (wd_h, wd_in),
            (cot_h, xc.at[mp]), (cos_h, cos_t), (sin_h, sin_t),
        ))
    ]
    for load in loads:
        load.start()

    def norm(vals):
        centered = vals - jnp.mean(vals, axis=-1, keepdims=True)
        inv = lax.rsqrt(jnp.mean(centered * centered, axis=-1, keepdims=True) + norm_eps)
        return centered * inv, inv

    def norm_back(grad, normed, inv, gain):
        scaled = grad * gain
        return inv * (
            scaled
            - jnp.mean(scaled, axis=-1, keepdims=True)
            - normed * jnp.mean(scaled * normed, axis=-1, keepdims=True)
        )

    def flip(vals):
        high, wide = vals.shape
        more_rows, more_cols = -high % 128, -wide % 128
        if more_cols:
            vals = jnp.concatenate([vals, jnp.zeros((high, more_cols), F32)], axis=1)
        if more_rows:
            vals = jnp.concatenate([vals, jnp.zeros((more_rows, wide + more_cols), F32)], axis=0)
        return vals.T[:wide, :high]

    def packed(q, k, v, o):
        parts = []
        for h in range(heads):
            parts += [q[:, h * HEAD_DIM : (h + 1) * HEAD_DIM], k[:, h * HEAD_DIM : (h + 1) * HEAD_DIM]]
        return jnp.concatenate([*parts, v, o], axis=1)

    gpad[...] = jnp.concatenate(
        [
            jnp.concatenate([gain_a[...].astype(F32), gain_b[...].astype(F32), jnp.zeros((6, shard), F32)], axis=0),
            jnp.zeros((8, 128 - shard), F32),
        ],
        axis=1,
    )
    loads[0].wait()
    loads[2].wait()
    w1[...] = packed(
        wq_in[0].astype(F32), wq_in[1].astype(F32), wq_in[2].astype(F32), flip(wo_in[...].astype(F32))
    ).astype(BF)
    loads[3].wait()
    loads[4].wait()
    w2[...] = jnp.concatenate(
        [
            wi_in[:, 0, :].astype(F32), wi_in[:, 1, :].astype(F32), flip(wd_in[...].astype(F32)),
            jnp.zeros((shard, cols_two - 3 * units), F32),
        ],
        axis=1,
    ).astype(BF)
    loads[1].wait()
    loads[5].wait()
    loads[6].wait()
    loads[7].wait()
    pl.semaphore_wait(barrier, ndp - 1 + 3)

    def gather_open(src, full, lo, hi):
        at = pl.ds(lo, hi - lo)
        return (src, full, at, [slot() for _ in range(na)], [slot() for _ in range(na)])

    def gather_far(state):
        src, full, at, zs, xs = state
        for k in (2, 1, 3):
            put(src.at[:, at], full.at[dp, :, at], zs[k], at_dp(lax.rem(za + k, na) * PAIR + zb))

    def gather_near(state):
        src, full, at, zs, xs = state
        put(src.at[:, at], full.at[dp, :, at], xs[0], at_dp(xpeer))

    def gather_forward(state, k):
        src, full, at, zs, xs = state
        source = lax.rem(za + na - k, na) * PAIR + zb
        got(full.at[source, :, at], zs[k])
        put(full.at[source, :, at], full.at[source, :, at], xs[k], at_dp(xpeer))

    def gather_end(state):
        src, full, at, zs, xs = state
        for k in range(na):
            source = lax.rem(za + na - k, na) * PAIR + (1 - zb)
            got(full.at[source, :, at], xs[k])

    order = (1, 3, 2)
    part_rows = rows // PARTS

    def part_at(p):
        return pl.ds(p * part_rows, part_rows)

    def spread_open(buf):
        return (buf, [[slot() for _ in range(3)] for _ in range(PARTS)])

    def spread_start(state, p):
        buf, sems = state
        block = buf.at[mp, part_at(p)]
        put(block, block, sems[p][0], at_mp(ypeer))
        put(block, block, sems[p][1], at_mp(mate))

    def spread_near(state):
        buf, sems = state
        for p in range(PARTS):
            got(buf.at[mate, part_at(p)], sems[p][1])

    def spread_forward(state, p):
        buf, sems = state
        block = buf.at[ypeer, part_at(p)]
        got(block, sems[p][0])
        put(block, block, sems[p][2], at_mp(mate))

    def spread_far(state):
        buf, sems = state
        for p in range(PARTS):
            got(buf.at[diag, part_at(p)], sems[p][2])

    def chunk(r):
        return pl.ds(pl.multiple_of(r * rows, rows), rows)

    def pair_rows(y):
        return pl.ds(pl.multiple_of(y * 2 * rows, 2 * rows), 2 * rows)

    near, far = pair_rows(ypos), pair_rows(1 - ypos)

    def pair_of(buf, y):
        return buf[pl.ds(pl.multiple_of(y * 2, 2), 2)].reshape(2 * rows, width)

    def scatter_open(i):
        return (i, [slot() for _ in range(PARTS)], slot(), [slot() for _ in range(PARTS)])

    def gain_part(part, x, r, row):
        if x is not None:
            gv[row : row + 1, :] += jnp.sum(part * x[r].astype(F32), axis=0, keepdims=True)

    def scatter_far(state, left, weights, x=None, row=0):
        i, s_far, s_near, s_y = state
        part = nt(left[chunk(diag), :], weights)
        rs_sc[i, 0] = part.astype(BF)
        for p in range(PARTS):
            at = part_at(p)
            put(rs_sc.at[i, 0, at], rs_rc.at[i, 0, at], s_far[p], at_mp(mate))
        gain_part(part, x, diag, row)
        part = nt(left[chunk(ypeer), :], weights)
        rs_own[i, 0] = part
        gain_part(part, x, ypeer, row)

    def scatter_send(state):
        i, s_far, s_near, s_y = state
        for p in range(PARTS):
            at = part_at(p)
            got(rs_rc.at[i, 0, at], s_far[p])
            rs_sy[i, at, :] = (rs_own[i, 0, at, :] + rs_rc[i, 0, at, :].astype(F32)).astype(BF)
            put(rs_sy.at[i, at], rs_ry.at[i, at], s_y[p], at_mp(ypeer))

    def scatter_near(state, left, weights, x=None, row=0):
        i, s_far, s_near, s_y = state
        part = nt(left[chunk(mate), :], weights)
        rs_sc[i, 1] = part.astype(BF)
        put(rs_sc.at[i, 1], rs_rc.at[i, 1], s_near, at_mp(mate))
        gain_part(part, x, mate, row)
        part = nt(left[chunk(mp), :], weights)
        rs_own[i, 1] = part
        gain_part(part, x, mp, row)

    def scatter_end(state, p):
        i, s_far, s_near, s_y = state
        at = part_at(p)
        if p == 0:
            got(rs_rc.at[i, 1], s_near)
        total = rs_own[i, 1, at, :] + rs_rc[i, 1, at, :].astype(F32)
        got(rs_ry.at[i, at], s_y[p])
        return total + rs_ry[i, at, :].astype(F32)

    def turn(buf, dst):
        @pl.loop(0, nmp)
        def _(r):
            cols = pl.ds(pl.multiple_of(r * rows, rows), rows)
            flipped = buf[r].T
            dst[:, :, :, cols] = flipped.reshape(na, PAIR, shard, rows)

    def product(xt, half, right):
        return nn(xt[:, half].reshape(na * shard, length), right).reshape(na, shard, right.shape[1])

    def grad_open(bufs, lo, hi):
        return (bufs, pl.ds(lo, hi - lo), [slot() for _ in range(na)], [slot() for _ in range(na)])

    def grad_start(state):
        (gs, gr, gz, gy, gw), at, xs, zs = state
        for k in (2, 1, 3, 0):
            a = lax.rem(za + k, na)
            put(gs.at[a, :, at], gr.at[a, :, at], xs[k], at_dp(xpeer))

    def grad_middle(state, k):
        (gs, gr, gz, gy, gw), at, xs, zs = state
        a = lax.rem(za + k, na)
        got(gr.at[a, :, at], xs[k])
        gz[k, :, at] = (gw[a, :, at] + gr[a, :, at].astype(F32)).astype(BF)
        put(gz.at[k, :, at], gy.at[k, :, at], zs[k], at_dp(a * PAIR + zb))

    def grad_end(state):
        (gs, gr, gz, gy, gw), at, xs, zs = state
        got(gr.at[za, :, at], xs[0])
        total = gw[za, :, at] + gr[za, :, at].astype(F32)
        for k in range(1, na):
            got(gy.at[k, :, at], zs[k])
            total = total + gy[k, :, at].astype(F32)
        return total

    one = (gs1, gr1, gz1, gy1, gw1)
    two = (gs2, gr2, gz2, gy2, gw2)

    gain_slots = [slot() for _ in range(ndp - 1)]
    for k in range(1, ndp):
        put(gpad, gains.at[dp], gain_slots[k - 1], at_dp(lax.rem(dp + k, ndp)))
    pieces = [gather_open(w1, wf1, c, c + 128) for c in range(0, cols_one, 128)]
    count_one = len(pieces)
    count_q = -(-3 * lw // 128)
    pieces += [gather_open(w2, wf2, c, c + 128) for c in range(0, cols_two, 128)]
    at_piece = [0]

    def pump(count):
        for _ in range(count):
            i = at_piece[0]
            if i >= len(pieces):
                return
            at_piece[0] += 1
            if i + AHEAD < len(pieces) and i < count_q:
                gather_far(pieces[i + AHEAD])
            if i + 1 < len(pieces) and i < count_q:
                gather_near(pieces[i + 1])
            for k in order:
                gather_forward(pieces[i], k)

    sp1 = spread_open(xr)
    gather_near(pieces[0])
    for i in range(AHEAD):
        gather_far(pieces[i])
        if i == 0:
            for p in range(PARTS):
                spread_start(sp1, p)
    gains[dp] = gpad[...]
    wf1[dp] = w1[...]
    wf2[dp] = w2[...]
    for k in range(1, ndp):
        source = lax.rem(dp + ndp - k, ndp)
        got(gains.at[source], gain_slots[k - 1])

    def whole_gain(i):
        return jnp.concatenate([gains[d, i : i + 1, :shard] for d in range(ndp)], axis=1)

    gain_one = whole_gain(0)
    gain_two = whole_gain(1)

    normed_one, inv_one = norm(xr[mp].astype(F32))
    xh1[...] = normed_one
    x1[mp] = (normed_one * gain_one).astype(BF)

    def first_norm(r):
        x1[r] = (norm(xr[r].astype(F32))[0] * gain_one).astype(BF)

    pump(1)
    spread_near(sp1)
    first_norm(mate)
    spc = spread_open(xc)
    pump(1)
    for p in range(PARTS):
        spread_forward(sp1, p)
        spread_start(spc, p)
    first_norm(ypeer)
    pump(1)
    spread_far(sp1)
    first_norm(diag)
    turn(x1, xt1)
    pump(count_q - 2)
    for p in range(PARTS):
        spread_forward(spc, p)
    for piece in pieces[count_q + AHEAD :]:
        gather_far(piece)
    for piece in pieces[count_q + 1 :]:
        gather_near(piece)
    for i in range(count_q):
        gather_end(pieces[i])

    wide[:, : 3 * lw] = nn(
        x1[...].reshape(length, width), wf1[:, :, : 3 * lw].reshape(width, 3 * lw)
    )

    @pl.loop(0, nmp)
    def _(r):
        at = chunk(r)
        for h in range(heads):
            t = slice(h * 128, (h + 1) * 128)
            u = wide[at, t]
            qk[at, t] = (u * cos_t[at, :] + swap_halves(u) * sin_t[at, :]).astype(BF)
        vb[at, :] = wide[at, 2 * lw : 3 * lw].astype(BF)

    scale = HEAD_DIM ** (-0.5)

    def query(h, at=slice(None)):
        return qk[at, h * 128 : h * 128 + HEAD_DIM]

    def key(h, at=slice(None)):
        return qk[at, h * 128 + HEAD_DIM : (h + 1) * 128]

    def value(h, at=slice(None)):
        return vb[at, h * HEAD_DIM : (h + 1) * HEAD_DIM]

    def attend(at):
        outs = []
        for h in range(heads):
            scores = nt(query(h, at), key(h)) * scale
            peak = jnp.max(scores, axis=-1, keepdims=True)
            e = jnp.exp(scores - peak)
            probs = e / jnp.sum(e, axis=-1, keepdims=True)
            pbuf[h, at, :] = probs
            outs.append(nn(probs.astype(BF), value(h)))
        att[at, :] = jnp.concatenate(outs, axis=1).astype(BF)

    pump(1)
    attend(far)
    pump(1)
    for i in range(count_q, count_one):
        gather_end(pieces[i])
    wof[...] = wf1[:, :, 3 * lw :].reshape(width, lw)
    rs_a = scatter_open(0)
    scatter_far(rs_a, att, wof[...])
    scatter_send(rs_a)
    attend(near)
    scatter_near(rs_a, att, wof[...])
    pump(1)
    spread_near(spc)
    spread_far(spc)
    turn(xc, xtc)
    pump(2)

    inv_two = []
    sp2 = spread_open(x2)
    for p in range(PARTS):
        at = part_at(p)
        mixed[at, :] = xr[mp, at, :].astype(F32) + scatter_end(rs_a, p)
        normed_two, inv = norm(mixed[at, :])
        inv_two.append(inv)
        xh2[at, :] = normed_two
        x2[mp, at, :] = (normed_two * gain_two).astype(BF)
        spread_start(sp2, p)
    def gelu_part(y, at):
        wide[at, : 2 * units] = nn(
            pair_of(x2, y), wf2[:, :, : 2 * units].reshape(width, 2 * units)
        )
        hgrad_buf[at, :] = nn(
            pair_of(xc, y), wf2[:, :, 2 * units : 3 * units].reshape(width, units)
        )

        @pl.loop(0, 2)
        def _(r):
            now = chunk(2 * y + r)
            u = wide[now, :units]
            gate = wide[now, units : 2 * units]
            cdf = 0.5 * (1.0 + erf(u * 0.7071067811865476))
            act = u * cdf
            slope = cdf + u * jnp.exp(-0.5 * u * u) * 0.3989422804014327
            hid[now, :] = (act * gate).astype(BF)
            hgrad = hgrad_buf[now, :]
            lg[now, :] = jnp.concatenate([hgrad * gate * slope, hgrad * act], axis=1).astype(BF)

    pump(1)
    spread_near(sp2)
    pump(1)
    for p in range(PARTS):
        spread_forward(sp2, p)
    spread_far(sp2)
    turn(x2, xt2)
    pump(len(pieces))
    for piece in pieces[count_one:]:
        gather_end(piece)
    gelu_part(ypos, near)
    gelu_part(1 - ypos, far)
    in_flat = wf2[:, :, : 2 * units].reshape(width, 2 * units)
    rs_g = scatter_open(1)
    gv[...] = jnp.zeros_like(gv)
    scatter_far(rs_g, lg, in_flat, x2, 1)
    g_two = [grad_open(two, c, c + 128) for c in range(0, cols_two, 128)]
    early = 2 * units // 128
    steps = []

    waiting = []
    flying = [0]

    def leave(state):
        steps.extend((state, k) for k in (2, 1, 3))
        if flying[0] < WINDOW:
            flying[0] += 1
            grad_start(state)
        else:
            waiting.append(state)

    def reduce_steps(count):
        for _ in range(min(count, len(steps))):
            state, k = steps.pop(0)
            grad_middle(state, k)
            if k == 3:
                if waiting:
                    grad_start(waiting.pop(0))
                else:
                    flying[0] -= 1

    gs2[:, :, : 2 * units] = product(xt2, 1 - zb, lg[...]).astype(BF)
    for g in g_two[:early]:
        leave(g)
    scatter_send(rs_g)
    gs2[:, :, 2 * units : 3 * units] = product(xtc, 1 - zb, hid[...]).astype(BF)
    gs2[:, :, 3 * units :] = jnp.zeros((na, shard, cols_two - 3 * units), BF)
    for g in g_two[early:]:
        leave(g)
    scatter_near(rs_g, lg, in_flat, x2, 1)
    gw2[:, :, : 2 * units] = product(xt2, zb, lg[...])
    gw2[:, :, 2 * units : 3 * units] = product(xtc, zb, hid[...])
    gw2[:, :, 3 * units :] = jnp.zeros((na, shard, cols_two - 3 * units), F32)
    down_flat = wf2[:, :, 2 * units : 3 * units].reshape(width, units)
    rs_o = scatter_open(3)
    scatter_far(rs_o, hid, down_flat)
    scatter_near(rs_o, hid, down_flat)
    reduce_steps(6)
    sp3 = spread_open(x3)
    for p in range(PARTS):
        at = part_at(p)
        back_two = norm_back(scatter_end(rs_g, p), xh2[at, :], inv_two[p], gain_two)
        mgrad[at, :] = xc[mp, at, :].astype(F32) + back_two
        x3[mp, at, :] = mgrad[at, :].astype(BF)
        spread_start(sp3, p)
    scatter_send(rs_o)
    reduce_steps(4)
    spread_near(sp3)

    def attend_back(y, at, h, first):
        g = gatt[at, h * HEAD_DIM : (h + 1) * HEAD_DIM]
        o = att[at, h * HEAD_DIM : (h + 1) * HEAD_DIM]
        probs = pbuf[h, at, :]
        dv = tn(probs.astype(BF), g)
        dprobs = nt(g, value(h))
        delta = jnp.sum(g.astype(F32) * o.astype(F32), axis=-1, keepdims=True)
        ds = (probs * (dprobs - delta) * scale).astype(BF)
        dqs[h, at, :] = nn(ds, key(h))
        dk = tn(ds, query(h, at))
        if first:
            dvs[h] = dv
            dks[h] = dk
        else:
            dvs[h] += dv
            dks[h] += dk

    gatt[near, :] = nn(pair_of(x3, ypos), wof[...]).astype(BF)
    for h in range(heads):
        attend_back(ypos, near, h, True)
        reduce_steps(1)
    for p in range(PARTS):
        spread_forward(sp3, p)
    reduce_steps(5)
    spread_far(sp3)
    gatt[far, :] = nn(pair_of(x3, 1 - ypos), wof[...]).astype(BF)
    turn(x3, xt3)
    late = -(-3 * lw // 128) * 128
    gs1[:, :, 3 * lw :] = product(xt3, 1 - zb, att[...]).astype(BF)
    g_one = {c: grad_open(one, c, c + 128) for c in range(0, cols_one, 128)}
    for c in range(late, cols_one, 128):
        leave(g_one[c])
    gw1[:, :, 3 * lw :] = product(xt3, zb, att[...])
    done = 2 * lw
    for h in range(heads):
        attend_back(1 - ypos, far, h, False)
        t = slice(h * 128, (h + 1) * 128)
        v = slice(2 * lw + h * HEAD_DIM, 2 * lw + (h + 1) * HEAD_DIM)

        @pl.loop(0, nmp)
        def _(r):
            at = chunk(r)
            u = jnp.concatenate([dqs[h, at, :], dks[h, at, :]], axis=1)
            pg[at, t] = (u * cos_t[at, :] - swap_halves(u) * sin_t[at, :]).astype(BF)
            pg[at, v] = dvs[h, at, :].astype(BF)

        gs1[:, :, t] = product(xt1, 1 - zb, pg[:, t]).astype(BF)
        leave(g_one[h * 128])
        last = h == heads - 1
        end = late if last else (2 * lw + (h + 1) * HEAD_DIM) // 128 * 128
        if end > done:
            ready = slice(done, min(end, 3 * lw))
            gs1[:, :, ready] = product(xt1, 1 - zb, pg[:, ready]).astype(BF)
            for c in range(done, end, 128):
                leave(g_one[c])
            gw1[:, :, ready] = product(xt1, zb, pg[:, ready])
            done = end
        gw1[:, :, t] = product(xt1, zb, pg[:, t])
        reduce_steps(2)

    qkv_flat = wf1[:, :, : 3 * lw].reshape(width, 3 * lw)
    rs_f = scatter_open(2)
    scatter_far(rs_f, pg, qkv_flat, x1, 0)
    reduce_steps(3)
    scatter_send(rs_f)
    scatter_near(rs_f, pg, qkv_flat, x1, 0)
    gain_sems = [slot() for _ in range(3)]
    for k, other in enumerate((ypeer, mate, diag)):
        put(gv, gvr.at[k], gain_sems[k], at_mp(other))
    reduce_steps(99)
    gain_sum = gv[...]
    for k in range(3):
        got(gvr.at[k], gain_sems[k])
        gain_sum = gain_sum + gvr[k]
    empty = jnp.zeros((8, 128 - shard), F32)
    for d in range(ndp):
        ggs[d] = jnp.concatenate([gain_sum[:, d * shard : (d + 1) * shard], empty], axis=1)
    sum_sems = [slot() for _ in range(ndp)]
    for k in range(1, ndp):
        d = lax.rem(dp + k, ndp)
        put(ggs.at[d], ggr.at[k], sum_sems[k], at_dp(d))

    for p in range(PARTS):
        at = part_at(p)
        out_o[at, :] = mixed[at, :] + scatter_end(rs_o, p)
    total_two = jnp.concatenate([grad_end(g) for g in g_two], axis=1)
    for i in range(2):
        di_o[:, i, :] = total_two[:, i * units : (i + 1) * units]
    dd_o[...] = flip(total_two[:, 2 * units : 3 * units])
    for p in range(PARTS):
        at = part_at(p)
        own_inv = inv_one[p * part_rows : (p + 1) * part_rows]
        back_one = norm_back(scatter_end(rs_f, p), xh1[at, :], own_inv, gain_one)
        tg_o[at, :] = mgrad[at, :] + back_one
    one_total = {c: grad_end(g) for c, g in sorted(g_one.items())}
    qk_total = [one_total[h * 128] for h in range(heads)]
    vo_total = jnp.concatenate([one_total[c] for c in range(2 * lw, cols_one, 128)], axis=1)
    dq_o[0] = jnp.concatenate([t[:, :HEAD_DIM] for t in qk_total], axis=1)
    dq_o[1] = jnp.concatenate([t[:, HEAD_DIM:] for t in qk_total], axis=1)
    dq_o[2] = vo_total[:, :lw]
    do_o[...] = flip(vo_total[:, lw:])
    total = ggs[dp]
    for k in range(1, ndp):
        got(ggr.at[k], sum_sems[k])
        total = total + ggr[k]
    ga_o[...] = total[0:1, :shard] / gain_a[...].astype(F32)
    gb_o[...] = total[1:2, :shard] / gain_b[...].astype(F32)
    for copy in sends:
        copy.wait_send()


def settle_kernel(*refs):
    count = (len(refs) - 1) // 2
    sems = refs[-1]
    copies = [
        pltpu.make_async_copy(src, dst, sems.at[i])
        for i, (src, dst) in enumerate(zip(refs[:count], refs[count:-1]))
    ]
    for copy in copies:
        copy.start()
    for copy in copies:
        copy.wait()


def fused_shards(tokens, cotangent, attn_gain, w_qkv, w_attn_out, mlp_gain, w_in, w_mlp_out):
    ndp = lax.axis_size("dp")
    nmp = lax.axis_size("mp")
    rows, width = tokens.shape
    shard = w_qkv.shape[0]
    lw = w_qkv.shape[2]
    units = w_in.shape[2]
    heads = lw // HEAD_DIM
    length = rows * nmp
    na = ndp // PAIR
    half = HEAD_DIM // 2
    cols_one = 4 * lw
    cols_two = -(-3 * units // 128) * 128
    freqs = rope_base ** (-(np.arange(half, dtype=np.float32) * np.float32(2.0) / HEAD_DIM))
    angles = np.arange(length, dtype=np.float32)[:, None] * freqs.astype(np.float32)[None, :]
    cos_t = np.tile(np.cos(angles).astype(np.float32), (1, 128 // half))
    sin = np.sin(angles).astype(np.float32)
    sin_t = np.tile(np.concatenate([-sin, sin], axis=1), (1, 128 // HEAD_DIM))

    def buf(shape, dtype=BF):
        return pltpu.VMEM(shape, dtype)

    def grad_bufs(cols):
        return [
            buf((na, shard, cols)), buf((na, shard, cols)), buf((na, shard, cols)),
            buf((na, shard, cols)), buf((na, shard, cols), F32),
        ]

    nsem = 2 * ndp + 2 * na * (cols_one + cols_two) // 128 + 4 * (3 * PARTS) + 4 * (2 * PARTS + 1) + 2 * na * (cols_one + cols_two) // 128 + 8
    scratch = [
        buf((3, shard, lw)), buf((lw, shard)), buf((shard, 2, units)), buf((units, shard)),
        buf((length, 128), F32), buf((length, 128), F32),
        buf((8, 128), F32), buf((ndp, 8, 128), F32),
        buf((shard, cols_one)), buf((shard, cols_two)),
        buf((ndp, shard, cols_one)), buf((ndp, shard, cols_two)), buf((width, lw)),
        *[buf((nmp, rows, width)) for _ in range(5)],
        *[buf((na, PAIR, shard, length)) for _ in range(4)],
        buf((length, heads * 128)), buf((length, lw)), buf((length, lw)),
        buf((heads, length, length), F32), buf((length, units)),
        buf((length, max(3 * lw, 2 * units)), F32), buf((length, units), F32),
        buf((length, 2 * units)), buf((length, 3 * lw)), buf((length, lw)),
        *[buf((heads, length, HEAD_DIM), F32) for _ in range(3)],
        *[buf((rows, width), F32) for _ in range(4)],
        buf((4, 2, rows, width)), buf((4, 2, rows, width)),
        buf((4, rows, width)), buf((4, rows, width)), buf((4, 2, rows, width), F32),
        *grad_bufs(cols_one), *grad_bufs(cols_two),
        buf((8, width), F32), buf((3, 8, width), F32), buf((ndp, 8, 128), F32), buf((ndp, 8, 128), F32),
        pltpu.SemaphoreType.DMA((nsem,)), pltpu.SemaphoreType.DMA((nsem,)),
        pltpu.SemaphoreType.DMA((8,)),
    ]
    vmem = pl.BlockSpec(memory_space=pltpu.VMEM)
    hbm = pl.BlockSpec(memory_space=pl.ANY)
    shapes = [
        (rows, width), (rows, width), (1, shard), (1, shard), (3, shard, lw), (lw, shard),
        (shard, 2, units), (units, shard),
    ]
    results = pl.pallas_call(
        functools.partial(layer_kernel, ndp, heads),
        out_shape=[buf(s, F32) for s in shapes],
        in_specs=[hbm, hbm, vmem, vmem, hbm, hbm, hbm, hbm, hbm, hbm],
        out_specs=[vmem] * 8,
        scratch_shapes=scratch,
        compiler_params=pltpu.CompilerParams(
            collective_id=0, has_side_effects=True, vmem_limit_bytes=56 * 1024 * 1024
        ),
    )(
        tokens, cotangent, attn_gain.reshape(1, shard), mlp_gain.reshape(1, shard),
        w_qkv.transpose(1, 0, 2), w_attn_out, w_in, w_mlp_out,
        jnp.asarray(cos_t), jnp.asarray(sin_t),
    )
    out, tg, ga, gb, dq, do, di, dd = pl.pallas_call(
        settle_kernel,
        out_shape=[jax.ShapeDtypeStruct(s, F32) for s in shapes],
        in_specs=[vmem] * 8,
        out_specs=[hbm] * 8,
        scratch_shapes=[pltpu.SemaphoreType.DMA((8,))],
    )(*[pltpu.with_memory_space_constraint(r, pltpu.VMEM) for r in results])
    return (
        out, tg, ga.reshape(shard), dq.transpose(1, 0, 2), do, gb.reshape(shard), di, dd,
    )


def choose(tokens, cotangent, attn_gain, w_qkv, w_attn_out, mlp_gain, w_in, w_mlp_out):
    ndp = lax.axis_size("dp")
    shard = w_qkv.shape[0]
    fits = (
        lax.axis_size("mp") == 4
        and ndp % PAIR == 0
        and shard % 16 == 0
        and shard <= 128
        and w_mlp_out.shape[1] == shard
        and tokens.shape[0] % 128 == 0
        and tokens.shape[0] <= 128
        and 4 * w_qkv.shape[2] % 128 == 0
        and w_qkv.shape[2] % HEAD_DIM == 0
    )
    form = fused_shards if fits else shards
    return form(tokens, cotangent, attn_gain, w_qkv, w_attn_out, mlp_gain, w_in, w_mlp_out)


def solution(mesh):
    in_specs = (
        P(("dp", "mp"), None),
        P(("dp", "mp"), None),
        P("dp"),
        P("dp", None, "mp"),
        P("mp", "dp"),
        P("dp"),
        P("dp", None, "mp"),
        P("mp", "dp"),
    )
    out_specs = (
        P(("dp", "mp"), None),
        P(("dp", "mp"), None),
        P("dp"),
        P("dp", None, "mp"),
        P("mp", "dp"),
        P("dp"),
        P("dp", None, "mp"),
        P("mp", "dp"),
    )
    return jax.shard_map(choose, mesh=mesh, in_specs=in_specs, out_specs=out_specs, check_vma=False)
```
